256 devices in a mesh: blk: 32 (over z, x), pair: 8 (over y, core).
Axes of the slice: x: 4, y: 4, z: 8, core: 2. Of those that a mesh axis runs over, the one named last changes fastest.
Arguments:
- amplitudes: bfloat16 [8, 384, 12, 1024], P('pair', 'blk'), may hold values from -6 to 6
- tile_mask: int32 [8, 384, 12], P('pair', 'blk'), may hold values 0 or 1
- integrals: bfloat16 [256, 1024, 1024], P('blk', 'pair'), may hold values from -0.0390625 to 0.0390625
- block_tiles: int32 [256, 2], P('blk'), may hold values from 0 to 11
- block_keep: int32 [256], P('blk'), may hold values 0 or 1
- slot_tile: int32 [96], replicated, may hold values from 0 to 95, each once
Outputs:
- ladder: bfloat16 [96, 8, 384, 128], P('blk', 'pair')
The draws below stay inside these ranges and needn't reach their ends.
Inputs may be any that keep to these rules, and one draw needn't show every extreme that they name: `slot_tile`: each result tile appears in exactly one slot.
All inputs are finite; a program needn't handle non-finite values. No bound on the sum of `tile_mask` or of `block_keep` on one device may be relied on, other than what follows from the above.
Results may differ from the reference program's by a relative error of at most 0.013.
Values may be sent and summed in bfloat16 or wider, within the bound.
A program may use at most 128 MiB of HBM per device.

```python
import jax
import jax.numpy as jnp
from jax import lax

TV = 128
NT = 12
DW = 8
BW = 8
KMAX = 8
SLABS = 8
SLAB_ROWS = 384
BLOCKS = 256
NOUT = 96
N_BLK = 32


def plant(values, rng, least, top_value):
    place = [jax.random.randint(jax.random.fold_in(rng, axis), (), 0, length) for axis, length in enumerate(values.shape)]
    longest = values.shape.index(max(values.shape))
    next_to = place[:longest] + [(place[longest] + 1) % values.shape[longest]] + place[longest + 1:]
    return values.at[tuple(place)].set(least).at[tuple(next_to)].set(top_value)


def block_scale(key, shape, pieces, low, top_value):
    loudness = 1.0
    for dim, blocks in pieces:
        draws = jax.random.uniform(jax.random.fold_in(jax.random.fold_in(key, 6), dim), (blocks,), jnp.float32, low / len(pieces), top_value / len(pieces))
        loudness = loudness * jnp.repeat(jnp.exp(draws), shape[dim] // blocks).reshape((-1,) + (1,) * (len(shape) - 1 - dim))
    return loudness


def scatter_about(stream_key, extent, deviation, reach, pieces=(), held_as=jnp.bfloat16):
    array = jax.random.normal(stream_key, extent, jnp.float32) * deviation
    if len(pieces) > 0:
        array = block_scale(stream_key, extent, pieces, -0.22, 0.18) * array
    return jnp.clip(array, min=-reach, max=reach).astype(held_as)


def setup_inputs(seed: int = 0) -> dict:
    splits = jax.random.split(jax.random.key(seed), 7)
    return {
        "amplitudes": scatter_about(splits[0], (SLABS, SLAB_ROWS, NT, DW * TV), 1.0, 6.0, ((0, 8), (1, 32))),
        "tile_mask": plant((jax.random.randint(splits[1], (SLABS, SLAB_ROWS, NT), 0, 4) < 3).astype(jnp.int32), jax.random.fold_in(splits[1], 1), 0, 1),
        "integrals": scatter_about(splits[2], (BLOCKS, DW * TV, BW * TV), (DW * TV * KMAX * N_BLK // NT) ** -0.5, 0.0390625, ((0, 32), (1, 8))),
        "block_tiles": plant(jax.random.randint(splits[3], (BLOCKS, 2), 0, NT), jax.random.fold_in(splits[3], 1), 0, NT - 1).astype(jnp.int32),
        "block_keep": plant((jax.random.randint(splits[4], (BLOCKS,), 0, 4) < 3).astype(jnp.int32), jax.random.fold_in(splits[4], 1), 0, 1),
        "slot_tile": jax.random.permutation(splits[5], NOUT).astype(jnp.int32),
    }


def reference(amplitudes, tile_mask, integrals, block_tiles, block_keep, slot_tile):
    masked = amplitudes * tile_mask.astype(jnp.bfloat16)[..., None]
    flattened = masked.reshape(SLABS * SLAB_ROWS, NT, DW * TV)

    def add_block(total, element):
        integral, pair_tiles, keep_flag = element
        row_block = lax.dynamic_index_in_dim(flattened, pair_tiles[0], 1, False)
        product = jnp.dot(row_block, integral, preferred_element_type=jnp.float32) * keep_flag.astype(jnp.float32)
        current = lax.dynamic_index_in_dim(total, pair_tiles[1], 1, False)
        return lax.dynamic_update_index_in_dim(total, current + product, pair_tiles[1], 1), None

    def add_holder(grand, element):
        begin = jnp.zeros((SLABS * SLAB_ROWS, NT, BW * TV), jnp.float32)
        holder_sum, _ = lax.scan(add_block, begin, element)
        rounded = lax.optimization_barrier(holder_sum.astype(jnp.bfloat16)).astype(jnp.float32)
        return grand + rounded, None

    grouped = (integrals.reshape(N_BLK, KMAX, DW * TV, BW * TV),
               block_tiles.reshape(N_BLK, KMAX, 2),
               block_keep.reshape(N_BLK, KMAX))
    grand = jnp.zeros((SLABS * SLAB_ROWS, NT, BW * TV), jnp.float32)
    grand, _ = lax.scan(add_holder, grand, grouped)
    tile_rows = grand.reshape(SLABS * SLAB_ROWS, NT * BW, TV)
    picked = jnp.take(tile_rows, slot_tile, axis=1)
    result = jnp.transpose(picked, (1, 0, 2)).reshape(NT * BW, SLABS, SLAB_ROWS, TV)
    return result.astype(jnp.bfloat16)
```

```python
import heapq

import jax
import jax.numpy as jnp
from jax import lax
from jax.experimental import pallas as pl
from jax.experimental.pallas import tpu as pltpu
from jax.sharding import Mesh
from jax.sharding import PartitionSpec as P

TV = 128
NT = 12
DW = 8
BW = 8
K = 8
D = DW * TV
ROWS = 384
NZ, NX, NY, NC = 8, 4, 4, 2
OWN = 3
RA, RB = 4, 8
ZERO = K * BW
MESH = pl.DeviceIdType.MESH
SIZE = {"z": NZ, "x": NX, "y": NY, "c": NC}

UNITS = (
    (0, 96, ("z", "x")),
    (96, 128, ("x", "z")),
    (224, 64, ("z", "x")),
    (288, 96, ("x", "z")),
)
CHUNKS = ((0, 2, 1), (2, 2, -1), (4, 1, 1), (5, 1, -1), (6, 1, 1), (7, 1, -1))

RATE = {"z": 45e3, "x": 45e3, "y": 45e3, "c": 150e3}
DELAY = {"z": 2.0, "x": 2.0, "y": 2.0, "c": 1.0}


class Plan:
    def __init__(self):
        self.tasks = []
        self.copies = {}

    def copy(self, name, axis, step, size, src, dst, got):
        self.copies[name] = (len(self.copies), axis, step, size, src, dst, got)

    def task(self, name, needs, run, sends, cost, rank=0.0):
        self.tasks.append((name, tuple(needs), run, tuple(sends), cost, rank))

    def order(self):
        known, waiting, ready, listing = {}, list(self.tasks), [], []
        free, now, count = {}, 0.0, 0
        while waiting or ready:
            rest = []
            for task in waiting:
                if all(need in known for need in task[1]):
                    when = max([known[need] for need in task[1]] + [0.0])
                    heapq.heappush(ready, (when + task[5], count, task))
                    count += 1
                else:
                    rest.append(task)
            waiting = rest
            _, _, task = heapq.heappop(ready)
            when = max([known[need] for need in task[1]] + [0.0])
            now = max(now, when) + task[4]
            known[task[0]] = now
            listing.append(task)
            for name in task[3]:
                _, axis, step, size, _, _, _ = self.copies[name]
                begin = max(now, free.get((axis, step), 0.0))
                free[axis, step] = begin + size / RATE[axis]
                known[name] = free[axis, step] + DELAY[axis]
        return listing, now


def messages(n, step):
    mine = 0 if step > 0 else 1
    listing = [(n // 2, mine)]
    for distance in range(n // 2 - 1, 0, -1):
        listing += [(distance, 1 - mine), (distance, mine)]
    return listing


def kernel(amps, integ, tiles, keep, slots, out, own_i, own_a, own_b, all_a, all_b, prod, final, perm, last, before, source, *rest):
    n_units = len(UNITS)
    recvs, stages, sums = rest[: 2 * n_units], rest[2 * n_units : 4 * n_units], rest[4 * n_units : 5 * n_units]
    send_sem, recv_sem, load_sem = rest[5 * n_units :]
    me = {axis: lax.axis_index(axis) for axis in SIZE}
    z, x, y, c = me["z"], me["x"], me["y"], me["c"]

    def shifted(axis, amount):
        return lax.rem(me[axis] + (amount + SIZE[axis]), SIZE[axis])

    loads = []
    for q, (first, count, _) in enumerate(CHUNKS):
        load = pltpu.make_async_copy(integ.at[pl.ds(first, count)], own_i.at[pl.ds(first, count), 2 * y + c], load_sem.at[q])
        load.start()
        loads.append(load)

    barrier = pltpu.get_barrier_semaphore()
    for axis, amount in (("z", 1), ("z", -1), ("x", 1), ("x", -1), ("y", 1), ("y", -1), ("c", 1)):
        pl.semaphore_signal(barrier, inc=1, device_id={axis: shifted(axis, amount)}, device_id_type=MESH)
    own_a[x] = amps[0 : NT * RA]
    own_b[z] = amps[NT * RA :]
    pl.semaphore_wait(barrier, 7)

    plan = Plan()

    def block(first, count, yy, core):
        return own_i.at[pl.ds(first, count), 2 * yy + core]

    all_i = []
    for q, (first, count, way) in enumerate(CHUNKS):
        size = count * TV * D * 2
        plan.task(f"load{q}", [], loads[q].wait, [], 0.05)
        for step in (1, -1):
            plan.copy(f"i{q}{step}", "y", step, size, block(first, count, y, c), block(first, count, y, c),
                      block(first, count, shifted("y", -step), c))
            needs = [f"i{q - 2}{step}"] if q >= 2 else []
            plan.task(f"si{q}{step}", needs + [f"load{q}"], None, [f"i{q}{step}"], 0.05, 0.01)
        far = shifted("y", -way)
        plan.copy(f"j{q}", "y", way, size, block(first, count, far, c), block(first, count, far, c),
                  block(first, count, shifted("y", 2), c))
        for tag, yy, need in (("o", y, f"load{q}"), ("p", shifted("y", -1), f"i{q}1"), ("m", shifted("y", 1), f"i{q}-1"), ("f", shifted("y", 2), f"j{q}")):
            plan.copy(f"c{q}{tag}", "c", 1, size, block(first, count, yy, c), block(first, count, yy, c),
                      block(first, count, yy, 1 - c))
            sends = [f"c{q}{tag}"]
            if tag == ("p" if way == 1 else "m"):
                sends = [f"j{q}"] + sends
            plan.task(f"sc{q}{tag}", [need], None, sends, 0.05)
        all_i.append([f"i{q}1", f"i{q}-1", f"j{q}"] + [f"c{q}{tag}" for tag in "opmf"])

    def gather(tag, axis, piece, size, need):
        n = SIZE[axis]
        names = []
        for step in (1, -1):
            for hop in range(n // 2):
                halves = (0, 1) if hop < n // 2 - 1 else ((0,) if step > 0 else (1,))
                for half in halves:
                    name = f"{tag}{step}.{hop}.{half}"
                    ref = piece(shifted(axis, -step * hop), half)
                    plan.copy(name, axis, step, size // 2, ref, ref, piece(shifted(axis, -step * (hop + 1)), half))
                    plan.task("s" + name, [f"{tag}{step}.{hop - 1}.{half}"] if hop else need, None, [name], 0.05)
                    names.append(name)
        return names

    got_a = gather("a", "x", lambda i, h: own_a.at[i, :, pl.ds(h * 512, 512)], NT * RA * D * 2, [])
    got_b = gather("b", "z", lambda i, h: own_b.at[i, :, pl.ds(h * 512, 512)], NT * RB * D * 2, [])

    def make_perm():
        to = lax.broadcasted_iota(jnp.int32, (192, 192), 0)
        fr = lax.broadcasted_iota(jnp.int32, (192, 192), 1)
        perm[...] = (fr == (to & 15) * NT + (to >> 4)).astype(jnp.float32).astype(jnp.bfloat16)
        prod[ZERO] = jnp.zeros((ROWS, TV), jnp.bfloat16)

    def make_tables():
        for a in range(NT):
            found = jnp.int32(K)
            for k in range(K):
                found = jnp.where((keep[k] != 0) & (tiles[k, 1] == a), k, found)
            last[a] = found
        for k in range(K):
            found = jnp.int32(K)
            for j in range(k):
                found = jnp.where((keep[j] != 0) & (tiles[j, 1] == tiles[k, 1]), j, found)
            before[k] = found

        def fill(s, carry):
            tile = slots[s]
            found = last[tile >> 3]
            source[s] = jnp.where(found == K, ZERO, found * BW + (tile & 7))
            return carry

        lax.fori_loop(0, NT * BW, fill, 0)

    plan.task("perm", [], make_perm, [], 0.5, 0.5)
    plan.task("tables", [], make_tables, [], 2.0, 6.0)

    def regroup(load, store):
        def tile(n, carry):
            cols = pl.ds(pl.multiple_of(n * 256, 256), 256)
            moved = jnp.dot(perm[...], load(cols), preferred_element_type=jnp.float32)
            store(cols, moved.astype(jnp.bfloat16).reshape(NT, 16, 256))
            return carry

        lax.fori_loop(0, D // 256, tile, 0)

    def regroup_a():
        def store(cols, value):
            all_a[z, :, :, cols] = value

        regroup(lambda cols: own_a[:, :, cols].reshape(192, 256), store)

    def regroup_b():
        for g in range(4):
            def store(cols, value):
                all_b[x, :, 16 * g : 16 * g + 16, cols] = value

            regroup(lambda cols: own_b[2 * g : 2 * g + 2, :, cols].reshape(192, 256), store)

    plan.task("ra", got_a + ["perm"], regroup_a, [], 0.5)
    plan.task("rb", got_b + ["perm"], regroup_b, [], 1.5)
    got_c = gather("u", "z", lambda i, h: all_a.at[i, pl.ds(h * 6, 6)], NT * 16 * D * 2, ["ra"])
    got_d = gather("v", "x", lambda i, h: all_b.at[i, pl.ds(h * 6, 6)], NT * 64 * D * 2, ["rb"])

    def multiply(first, count):
        def tile(t, carry):
            k = first + lax.div(t, 4)
            n = lax.rem(t, 4)
            cols = pl.ds(pl.multiple_of(n * 256, 256), 256)
            which = tiles[k, 0]
            lhs = jnp.concatenate([all_a[:, which].reshape(NZ * 16, D), all_b[:, which].reshape(NX * 64, D)], axis=0)
            value = jnp.dot(lhs, own_i[k, :, :, cols].reshape(D, 256), preferred_element_type=jnp.float32)
            found = before[k]
            for half in range(2):
                b = 2 * n + half
                old = prod[jnp.where(found == K, ZERO, found * BW + b)].astype(jnp.float32)
                prod[k * BW + b] = (value[:, half * TV : half * TV + TV] + old).astype(jnp.bfloat16)
            return carry

        lax.fori_loop(0, 4 * count, tile, 0)

    for q, (first, count, _) in enumerate(CHUNKS):
        needs = all_i[q] + got_c + got_d + ["tables"] + ([f"mm{q - 1}"] if q else [])
        plan.task(f"mm{q}", needs, lambda first=first, count=count: multiply(first, count), [], 1.3 * count)

    def reduce(tag, axis, count, rows, own, recv, stage, sink, need):
        n = SIZE[axis]
        size = count * rows * TV * 2
        for step in (1, -1):
            d = 0 if step > 0 else 1
            listing = messages(n, step)
            for m, (distance, half) in enumerate(listing):
                name = f"{tag}{step}.{distance}.{half}"
                dest = shifted(axis, step * distance)
                upstream = (distance + 1, half)
                if upstream in listing:
                    buf = recv.at[d, listing.index(upstream)]
                    needs = [f"{tag}{step}.{distance + 1}.{half}"]

                    def run(buf=buf, dest=dest, half=half):
                        def one(i, carry):
                            buf[i] = (buf[i].astype(jnp.float32) + own(dest, i, half).astype(jnp.float32)).astype(jnp.bfloat16)
                            return carry

                        lax.fori_loop(0, count, one, 0)
                else:
                    buf = stage.at[d, m]
                    needs = []

                    def run(buf=buf, dest=dest, half=half):
                        def one(i, carry):
                            buf[i] = own(dest, i, half)
                            return carry

                        lax.fori_loop(0, count, one, 0)

                plan.copy(name, axis, step, size, buf, recv.at[d, m], recv.at[d, m])
                plan.task("s" + name, needs + need, run, [name], count * rows / 2000.0)
        index = {step: messages(n, step) for step in (1, -1)}
        for half in range(2):
            def run(half=half):
                def one(i, carry):
                    total = own(me[axis], i, half).astype(jnp.float32)
                    total += recv[0, index[1].index((1, half)), i].astype(jnp.float32)
                    total += recv[1, index[-1].index((1, half)), i].astype(jnp.float32)
                    sink(i, half, total.astype(jnp.bfloat16))
                    return carry

                lax.fori_loop(0, count, one, 0)

            plan.task(f"f{tag}{half}", [f"{tag}1.1.{half}", f"{tag}-1.1.{half}"] + need, run, [], count * rows / 1500.0)
        return [f"f{tag}0", f"f{tag}1"]

    finals = []
    for u, (row, rows, axes) in enumerate(UNITS):
        half_rows = rows // 2
        summed = sums[u]

        if axes[0] == "z":
            count = NX * OWN

            def own1(dest, i, half, row=row, h=half_rows):
                return prod[source[dest * (NX * OWN) + i], row + half * h : row + half * h + h, :]
        else:
            count = NZ * OWN

            def own1(dest, i, half, row=row, h=half_rows):
                slot = lax.div(i, OWN) * (NX * OWN) + dest * OWN + lax.rem(i, OWN)
                return prod[source[slot], row + half * h : row + half * h + h, :]

        def sink1(i, half, value, summed=summed, h=half_rows):
            summed[i, half * h : half * h + h, :] = value

        def own2(dest, i, half, summed=summed, h=half_rows):
            return summed[dest * OWN + i, half * h : half * h + h, :]

        def sink2(i, half, value, row=row, h=half_rows):
            final[i, row + half * h : row + half * h + h, :] = value

        done = reduce(f"r{u}", axes[0], count, half_rows, own1, recvs[2 * u], stages[2 * u], sink1, [f"mm{len(CHUNKS) - 1}"])
        finals += reduce(f"t{u}", axes[1], OWN, half_rows, own2, recvs[2 * u + 1], stages[2 * u + 1], sink2, done)

    def finish():
        to = lax.broadcasted_iota(jnp.int32, (ROWS, ROWS), 0)
        p = lax.broadcasted_iota(jnp.int32, (ROWS, ROWS), 1)
        q = p - NZ * 16
        in_a = (p >> 4) * (NX * NT) + ((p >> 2) & 3) * NT + (p & 3)
        in_b = ((q >> 3) & 7) * (NX * NT) + (q >> 6) * NT + RA + (q & 7)
        place = (to == jnp.where(p < NZ * 16, in_a, in_b)).astype(jnp.float32).astype(jnp.bfloat16)
        for j in range(OWN):
            out[j] = jnp.dot(place, final[j], preferred_element_type=jnp.float32).astype(jnp.bfloat16)

    plan.task("finish", finals, finish, [], 1.0)

    listing, _ = plan.order()
    waited = set()

    def handle(name, received):
        number, axis, step, _, src, dst, got = plan.copies[name]
        return pltpu.make_async_remote_copy(
            src_ref=src, dst_ref=got if received else dst, send_sem=send_sem.at[number], recv_sem=recv_sem.at[number],
            device_id={axis: shifted(axis, step)}, device_id_type=MESH)

    for _, needs, run, sends, _, _ in listing:
        for need in needs:
            if need in plan.copies and need not in waited:
                waited.add(need)
                handle(need, True).wait_recv()
        if run is not None:
            run()
        for name in sends:
            handle(name, False).start()
    for name in plan.copies:
        if name not in waited:
            handle(name, True).wait_recv()
        handle(name, False).wait_send()


def scratch_shapes():
    bf = jnp.bfloat16
    shapes = [
        pltpu.VMEM((K, DW, TV, D), bf),
        pltpu.VMEM((NX, NT * RA, D), bf),
        pltpu.VMEM((NZ, NT * RB, D), bf),
        pltpu.VMEM((NZ, NT, 16, D), bf),
        pltpu.VMEM((NX, NT, 64, D), bf),
        pltpu.VMEM((ZERO + 1, ROWS, TV), bf),
        pltpu.VMEM((OWN, ROWS, TV), bf),
        pltpu.VMEM((192, 192), bf),
        pltpu.SMEM((NT,), jnp.int32),
        pltpu.SMEM((K,), jnp.int32),
        pltpu.SMEM((NT * BW,), jnp.int32),
    ]
    recv, stage, sums = [], [], []
    copies = 7 * len(CHUNKS) + 2 * (6 + 14)
    for _, rows, axes in UNITS:
        first = SIZE[axes[1]] * OWN
        for axis, count in zip(axes, (first, OWN)):
            recv.append(pltpu.VMEM((2, SIZE[axis] - 1, count, rows // 2, TV), bf))
            stage.append(pltpu.VMEM((2, 2, count, rows // 2, TV), bf))
            copies += 2 * (SIZE[axis] - 1)
        sums.append(pltpu.VMEM((first, rows, TV), bf))
    sems = [pltpu.SemaphoreType.DMA((copies,)), pltpu.SemaphoreType.DMA((copies,)), pltpu.SemaphoreType.DMA((len(CHUNKS),))]
    return shapes + recv + stage + sums + sems


def per_device(amplitudes, tile_mask, integrals, block_tiles, block_keep, slot_tile):
    masked = amplitudes[0] * tile_mask[0].astype(jnp.bfloat16)[:, :, None]
    rows, tile_count, depth = masked.shape
    vmem, smem = pl.BlockSpec(memory_space=pltpu.VMEM), pl.BlockSpec(memory_space=pltpu.SMEM)
    ladder = pl.pallas_call(
        kernel,
        out_shape=jax.ShapeDtypeStruct((OWN, ROWS, TV), jnp.bfloat16),
        in_specs=[vmem, pl.BlockSpec(memory_space=pl.ANY), smem, smem, smem],
        out_specs=vmem,
        scratch_shapes=scratch_shapes(),
        compiler_params=pltpu.CompilerParams(collective_id=0, has_side_effects=True, vmem_limit_bytes=67043328),
        name="ladder",
    )(masked.reshape(rows * tile_count, depth), integrals, block_tiles, block_keep, slot_tile)
    return ladder[:, None]


def solution(mesh):
    torus = Mesh(mesh.devices.reshape(NZ, NX, NY, NC), ("z", "x", "y", "c"))
    blk, pair = ("z", "x"), ("y", "c")
    return jax.shard_map(
        per_device,
        mesh=torus,
        in_specs=(P(pair, blk, None, None), P(pair, blk, None), P(blk, pair, None), P(blk, None), P(blk), P()),
        out_specs=P(blk, pair, None, None),
        check_vma=False,
    )
```

```python
import jax
import jax.numpy as jnp
from jax import lax
from jax.experimental import pallas as pl
from jax.experimental.pallas import tpu as pltpu
from jax.sharding import Mesh
from jax.sharding import PartitionSpec as P

TV = 128
NT = 12
DW = 8
BW = 8
K = 8
D = DW * TV
ROWS = 384
NZ, NX, NY, NC = 8, 4, 4, 2
OWN = 3
RG = 4
GROUPS = (("z", "x"), ("x", "z"), ("z", "x"))
ZERO = K * BW
MESH = pl.DeviceIdType.MESH
SIZE = {"z": NZ, "x": NX, "y": NY, "c": NC}

UNITS = (
    (0, 64, ("z", "x")),
    (64, 128, ("x", "z")),
    (192, 96, ("z", "x")),
    (288, 96, ("x", "z")),
)
RANK_OWN = (0.0, 0.0, 1.0)
RANK_ALL = (2.0, 4.0, 3.0)
AFTER_OWN = ([], [], ["a01.1.0"])
AFTER_ALL = ([], ["a21.2.0"], [])
RANK_FIRST = (0.0, 1.0, 2.0, 3.0)
RANK_SECOND = (4.0, 5.0, 6.0, 7.0)
CHUNKS = (
    (0, 0, 2, 1), (0, 2, 2, -1), (0, 4, 2, 1), (0, 6, 2, -1),
    (1, 0, 2, 1), (1, 2, 2, -1), (1, 4, 1, 1), (1, 5, 1, -1), (1, 6, 1, 1), (1, 7, 1, -1),
)

RATE = {"z": 45e3, "x": 45e3, "y": 45e3, "c": 150e3}
AHEAD = 3.0
DELAY = {"z": 2.0, "x": 2.0, "y": 2.0, "c": 1.0}


class Plan:
    def __init__(self):
        self.tasks = []
        self.copies = {}

    def copy(self, name, axis, step, size, src, dst, got):
        self.copies[name] = (len(self.copies), axis, step, size, src, dst, got)

    def task(self, name, needs, run, sends, cost, rank=0.0):
        self.tasks.append((name, tuple(needs), run, tuple(sends), cost, rank))

    def order(self):
        known, waiting, listing, free, now = {}, list(self.tasks), [], {}, 0.0
        while waiting:
            best = None
            for place, task in enumerate(waiting):
                if all(need in known for need in task[1]):
                    when = max([known[need] for need in task[1]] + [now])
                    for name in task[3]:
                        _, axis, step, _, _, _, _ = self.copies[name]
                        when = max(when, free.get((axis, step), 0.0) - AHEAD)
                    key = (when, task[5], place)
                    if best is None or key < best:
                        best = key
            when, _, place = best
            task = waiting.pop(place)
            now = when + task[4]
            known[task[0]] = now
            listing.append(task)
            for name in task[3]:
                _, axis, step, size, _, _, _ = self.copies[name]
                begin = max(now, free.get((axis, step), 0.0))
                free[axis, step] = begin + size / RATE[axis]
                known[name] = free[axis, step] + DELAY[axis]
        return listing, now


def messages(n, step):
    mine = 0 if step > 0 else 1
    listing = [(n // 2, mine)]
    for distance in range(n // 2 - 1, 0, -1):
        listing += [(distance, 1 - mine), (distance, mine)]
    return listing


def kernel(amps, integ, tiles, keep, slots, out, fresh, own_i, own_0, own_1, own_2, all_0, all_1, all_2, prod, final, perm, turn, last, before, source, *rest):
    n_units = len(UNITS)
    recvs, stages, sums = rest[: 2 * n_units], rest[2 * n_units : 4 * n_units], rest[4 * n_units : 5 * n_units]
    send_sem, recv_sem, load_sem = rest[5 * n_units :]
    me = {axis: lax.axis_index(axis) for axis in SIZE}
    z, x, y, c = me["z"], me["x"], me["y"], me["c"]

    def shifted(axis, amount):
        return lax.rem(me[axis] + (amount + SIZE[axis]), SIZE[axis])

    loads = []
    for k in range(0, K, 2):
        load = pltpu.make_async_copy(integ.at[pl.ds(k, 2)], fresh.at[pl.ds(k, 2)], load_sem.at[k // 2])
        load.start()
        loads.append(load)

    barrier = pltpu.get_barrier_semaphore()
    for axis, amount in (("z", 1), ("z", -1), ("x", 1), ("x", -1), ("y", 1), ("y", -1), ("c", 1)):
        pl.semaphore_signal(barrier, inc=1, device_id={axis: shifted(axis, amount)}, device_id_type=MESH)
    own, every = (own_0, own_1, own_2), (all_0, all_1, all_2)
    for g, (axis, _) in enumerate(GROUPS):
        own[g][me[GROUPS[g][1]], me[axis]] = amps[NT * RG * g : NT * RG * (g + 1)]
    fr = lax.broadcasted_iota(jnp.int32, (256, 256), 0)
    to = lax.broadcasted_iota(jnp.int32, (256, 256), 1)
    want = ((to >> 6) & 1) * 128 + (to >> 7) * 64 + (to & 63)
    turn[...] = (fr == want).astype(jnp.float32).astype(jnp.bfloat16)
    pl.semaphore_wait(barrier, 7)

    plan = Plan()

    def block(half, first, count, yy, core):
        return own_i.at[half, pl.ds(first, count), 2 * yy + core]

    def split(k):
        loads[k // 2].wait()

        def tile(t, carry):
            kk = k + lax.div(t, 4)
            j = lax.rem(t, 4)
            cols = pl.ds(pl.multiple_of(j * 256, 256), 256)
            moved = jnp.dot(fresh[kk, :, cols], turn[...], preferred_element_type=jnp.float32).astype(jnp.bfloat16)
            place = pl.ds(pl.multiple_of(j * TV, TV), TV)
            own_i[0, kk, 2 * y + c, :, place] = moved[:, :TV]
            own_i[1, kk, 2 * y + c, :, place] = moved[:, TV:]
            return carry

        lax.fori_loop(0, 8, tile, 0)

    for k in range(0, K, 2):
        plan.task(f"split{k}", [], lambda k=k: split(k), [], 0.4, 0.5 + k)

    all_i = []
    for q, (half, first, count, way) in enumerate(CHUNKS):
        size = count * TV * D
        for step in (1, -1):
            plan.copy(f"i{q}{step}", "y", step, size, block(half, first, count, y, c), block(half, first, count, y, c),
                      block(half, first, count, shifted("y", -step), c))
            needs = [f"i{q - 2}{step}"] if q >= 2 else []
            plan.task(f"si{q}{step}", needs + [f"split{first // 2 * 2}"], None, [f"i{q}{step}"], 0.05)
        far = shifted("y", -way)
        plan.copy(f"j{q}", "y", way, size, block(half, first, count, far, c), block(half, first, count, far, c),
                  block(half, first, count, shifted("y", 2), c))
        for tag, yy, need in (("o", y, f"split{first // 2 * 2}"), ("p", shifted("y", -1), f"i{q}1"), ("m", shifted("y", 1), f"i{q}-1"), ("f", shifted("y", 2), f"j{q}")):
            plan.copy(f"c{q}{tag}", "c", 1, size, block(half, first, count, yy, c), block(half, first, count, yy, c),
                      block(half, first, count, yy, 1 - c))
            sends = [f"c{q}{tag}"]
            if tag == ("p" if way == 1 else "m"):
                sends = [f"j{q}"] + sends
            plan.task(f"sc{q}{tag}", [need], None, sends, 0.05, 9.0 if tag == "o" else 0.0)
        all_i.append([f"i{q}1", f"i{q}-1", f"j{q}"] + [f"c{q}{tag}" for tag in "opmf"])

    arrived = []
    for g, (first, second) in enumerate(GROUPS):
        n, m = SIZE[first], SIZE[second]
        size = NT * RG * D * 2
        parts = {0: []}
        for step in (1, -1):
            for hop in range(n // 2):
                for half in (0, 1) if hop < n // 2 - 1 else ((0,) if step > 0 else (1,)):
                    name = f"a{g}{step}.{hop}.{half}"

                    def piece(offset, half=half, g=g, first=first, second=second):
                        return own[g].at[me[second], shifted(first, offset), :, pl.ds(half * 512, 512)]

                    ref = piece(-step * hop)
                    plan.copy(name, first, step, size // 2, ref, ref, piece(-step * (hop + 1)))
                    plan.task("s" + name, [f"a{g}{step}.{hop - 1}.{half}"] if hop else AFTER_OWN[g], None, [name], 0.05, RANK_OWN[g])
                    offset = -step * (hop + 1)
                    parts.setdefault(n // 2 if offset == -(n // 2) else offset, []).append(name)
        whole = {0: sum(parts.values(), [])}
        for number, offset in enumerate(sorted(parts, key=abs)):
            way = 1 if number % 2 == 0 else -1

            def piece(along, g=g, first=first, second=second, offset=offset):
                return own[g].at[shifted(second, along), shifted(first, offset)]

            for step in (1, -1):
                for hop in range(m // 2 if step == way else m // 2 - 1):
                    name = f"b{g}.{offset}.{step}.{hop}"
                    ref = piece(-step * hop)
                    plan.copy(name, second, step, size, ref, ref, piece(-step * (hop + 1)))
                    needs = [f"b{g}.{offset}.{step}.{hop - 1}"] if hop else parts[offset] + AFTER_ALL[g]
                    plan.task("s" + name, needs, None, [name], 0.05, RANK_ALL[g] + (0.0 if hop else 0.5))
                    along = -step * (hop + 1)
                    whole.setdefault(m // 2 if along == -(m // 2) else along, []).append(name)
        arrived.append(whole)

    def make_perm():
        to = lax.broadcasted_iota(jnp.int32, (192, 192), 0)
        fr = lax.broadcasted_iota(jnp.int32, (192, 192), 1)
        perm[...] = (fr == (to & 15) * NT + (to >> 4)).astype(jnp.float32).astype(jnp.bfloat16)
        prod[ZERO] = jnp.zeros((ROWS, TV), jnp.bfloat16)

    def make_tables():
        for a in range(NT):
            found = jnp.int32(K)
            for k in range(K):
                found = jnp.where((keep[k] != 0) & (tiles[k, 1] == a), k, found)
            last[a] = found
        for k in range(K):
            found = jnp.int32(K)
            for j in range(k):
                found = jnp.where((keep[j] != 0) & (tiles[j, 1] == tiles[k, 1]), j, found)
            before[k] = found

        def fill(s, carry):
            tile = slots[s]
            found = last[tile >> 3]
            source[s] = jnp.where(found == K, ZERO, found * BW + (tile & 7))
            return carry

        lax.fori_loop(0, NT * BW, fill, 0)

    plan.task("perm", [], make_perm, [], 0.5, 5.0)
    plan.task("tables", [], make_tables, [], 2.0, 90.0)

    def regroup(load, store):
        def tile(n, carry):
            cols = pl.ds(pl.multiple_of(n * 256, 256), 256)
            moved = jnp.dot(perm[...], load(cols), preferred_element_type=jnp.float32)
            store(cols, moved.astype(jnp.bfloat16).reshape(NT, 16, 256))
            return carry

        lax.fori_loop(0, D // 256, tile, 0)

    def regroup_block(g, along):
        first, second = GROUPS[g]
        there = shifted(second, along)
        for part in range(SIZE[first] // 4):
            def store(cols, value):
                every[g][there, :, 16 * part : 16 * part + 16, cols] = value

            regroup(lambda cols: own[g][there, 4 * part : 4 * part + 4, :, cols].reshape(192, 256), store)

    regrouped = []
    for g, (first, second) in enumerate(GROUPS):
        for along, names in arrived[g].items():
            plan.task(f"regroup{g}.{along}", names + ["perm"], lambda g=g, along=along: regroup_block(g, along), [], 0.25 * (SIZE[first] // 4), 6.0)
            regrouped.append(f"regroup{g}.{along}")

    lane = lax.broadcasted_iota(jnp.int32, (ROWS // 2, TV), 1)

    def multiply(part, first, count):
        rows = pl.ds(part * (ROWS // 2), ROWS // 2)

        def tile(t, carry):
            k = first + lax.div(t, 2)
            n = lax.rem(t, 2)
            cols = pl.ds(pl.multiple_of(n * 256, 256), 256)
            which = tiles[k, 0]
            lhs = jnp.concatenate([ref[:, which].reshape(NZ * NX * RG, D) for ref in every], axis=0)
            value = jnp.dot(lhs, own_i[part, k, :, :, cols].reshape(D, 256), preferred_element_type=jnp.float32)
            found = before[k]
            for pair in range(2):
                upper = value[: ROWS // 2, pair * TV : pair * TV + TV]
                lower = value[ROWS // 2 :, pair * TV : pair * TV + TV]
                packed = (
                    jnp.where(lane < 64, upper, pltpu.roll(lower, 64, 1)),
                    jnp.where(lane < 64, pltpu.roll(upper, 64, 1), lower),
                )
                for side in range(2):
                    b = 4 * n + 2 * pair + side
                    old = prod[jnp.where(found == K, ZERO, found * BW + b), rows, :].astype(jnp.float32)
                    prod[k * BW + b, rows, :] = (packed[side] + old).astype(jnp.bfloat16)
            return carry

        lax.fori_loop(0, 2 * count, tile, 0)

    multiplied = {}
    for q, (part, first, count, _) in enumerate(CHUNKS):
        needs = all_i[q] + regrouped + ["tables"] + ([multiplied[part]] if part in multiplied else [])
        plan.task(f"mm{q}", needs, lambda part=part, first=first, count=count: multiply(part, first, count), [], 0.8 * count, 8.0 * part - 1.0)
        multiplied[part] = f"mm{q}"

    def reduce(tag, axis, count, rows, own, recv, stage, sink, need, rank):
        n = SIZE[axis]
        size = count * rows * TV * 2
        for step in (1, -1):
            d = 0 if step > 0 else 1
            listing = messages(n, step)
            for m, (distance, half) in enumerate(listing):
                name = f"{tag}{step}.{distance}.{half}"
                dest = shifted(axis, step * distance)
                upstream = (distance + 1, half)
                if upstream in listing:
                    buf = recv.at[d, listing.index(upstream)]
                    needs = [f"{tag}{step}.{distance + 1}.{half}"]

                    def run(buf=buf, dest=dest, half=half):
                        def one(i, carry):
                            buf[i] = (buf[i].astype(jnp.float32) + own(dest, i, half).astype(jnp.float32)).astype(jnp.bfloat16)
                            return carry

                        lax.fori_loop(0, count, one, 0)
                else:
                    buf = stage.at[d, m]
                    needs = []

                    def run(buf=buf, dest=dest, half=half):
                        def one(i, carry):
                            buf[i] = own(dest, i, half)
                            return carry

                        lax.fori_loop(0, count, one, 0)

                plan.copy(name, axis, step, size, buf, recv.at[d, m], recv.at[d, m])
                plan.task("s" + name, needs + need, run, [name], count * rows / 2000.0, rank)
        index = {step: messages(n, step) for step in (1, -1)}
        for half in range(2):
            def run(half=half):
                def one(i, carry):
                    total = own(me[axis], i, half).astype(jnp.float32)
                    total += recv[0, index[1].index((1, half)), i].astype(jnp.float32)
                    total += recv[1, index[-1].index((1, half)), i].astype(jnp.float32)
                    sink(i, half, total.astype(jnp.bfloat16))
                    return carry

                lax.fori_loop(0, count, one, 0)

            plan.task(f"f{tag}{half}", [f"{tag}1.1.{half}", f"{tag}-1.1.{half}"] + need, run, [], count * rows / 1500.0, rank)
        return [f"f{tag}0", f"f{tag}1"]

    finals = []
    for u, (row, rows, axes) in enumerate(UNITS):
        half_rows = rows // 2
        summed = sums[u]

        if axes[0] == "z":
            count = NX * OWN

            def own1(dest, i, half, row=row, h=half_rows):
                return prod[source[dest * (NX * OWN) + i], row + half * h : row + half * h + h, :]
        else:
            count = NZ * OWN

            def own1(dest, i, half, row=row, h=half_rows):
                slot = lax.div(i, OWN) * (NX * OWN) + dest * OWN + lax.rem(i, OWN)
                return prod[source[slot], row + half * h : row + half * h + h, :]

        def sink1(i, half, value, summed=summed, h=half_rows):
            summed[i, half * h : half * h + h, :] = value

        def own2(dest, i, half, summed=summed, h=half_rows):
            return summed[dest * OWN + i, half * h : half * h + h, :]

        def sink2(i, half, value, row=row, h=half_rows):
            final[i, row + half * h : row + half * h + h, :] = value

        done = reduce(f"r{u}", axes[0], count, half_rows, own1, recvs[2 * u], stages[2 * u], sink1, [multiplied[row // (ROWS // 2)]], RANK_FIRST[u])
        finals += reduce(f"t{u}", axes[1], OWN, half_rows, own2, recvs[2 * u + 1], stages[2 * u + 1], sink2, done, RANK_SECOND[u])

    def finish():
        to = lax.broadcasted_iota(jnp.int32, (ROWS, ROWS), 0)
        p = lax.broadcasted_iota(jnp.int32, (ROWS, ROWS), 1)
        natural = jnp.zeros_like(p)
        for g, (first, _) in enumerate(GROUPS):
            q = p - g * NZ * NX * RG
            zz, xx = ((q >> 2) & 7, q >> 5) if first == "z" else (q >> 4, (q >> 2) & 3)
            natural = jnp.where(q >= 0, zz * (NX * NT) + xx * NT + g * RG + (q & 3), natural)
        place = (to == natural).astype(jnp.float32).astype(jnp.bfloat16)
        for j in range(OWN):
            left = final[j, : ROWS // 2].astype(jnp.float32)
            right = final[j, ROWS // 2 :].astype(jnp.float32)
            upper = jnp.where(lane < 64, left, pltpu.roll(right, 64, 1))
            lower = jnp.where(lane < 64, pltpu.roll(left, 64, 1), right)
            whole = jnp.concatenate([upper, lower], axis=0).astype(jnp.bfloat16)
            out[j] = jnp.dot(place, whole, preferred_element_type=jnp.float32).astype(jnp.bfloat16)

    plan.task("finish", finals, finish, [], 1.0)

    listing, _ = plan.order()
    waited = set()

    def handle(name, received):
        number, axis, step, _, src, dst, got = plan.copies[name]
        return pltpu.make_async_remote_copy(
            src_ref=src, dst_ref=got if received else dst, send_sem=send_sem.at[number], recv_sem=recv_sem.at[number],
            device_id={axis: shifted(axis, step)}, device_id_type=MESH)

    for _, needs, run, sends, _, _ in listing:
        for need in needs:
            if need in plan.copies and need not in waited:
                waited.add(need)
                handle(need, True).wait_recv()
        if run is not None:
            run()
        for name in sends:
            handle(name, False).start()
    for name in plan.copies:
        if name not in waited:
            handle(name, True).wait_recv()
        handle(name, False).wait_send()


def scratch_shapes():
    bf = jnp.bfloat16
    shapes = [
        pltpu.VMEM((K, TV, D), bf),
        pltpu.VMEM((2, K, DW, TV, D // 2), bf),
        *[pltpu.VMEM((SIZE[second], SIZE[first], NT * RG, D), bf) for first, second in GROUPS],
        *[pltpu.VMEM((SIZE[second], NT, SIZE[first] * RG, D), bf) for first, second in GROUPS],
        pltpu.VMEM((ZERO + 1, ROWS, TV), bf),
        pltpu.VMEM((OWN, ROWS, TV), bf),
        pltpu.VMEM((192, 192), bf),
        pltpu.VMEM((256, 256), bf),
        pltpu.SMEM((NT,), jnp.int32),
        pltpu.SMEM((K,), jnp.int32),
        pltpu.SMEM((NT * BW,), jnp.int32),
    ]
    recv, stage, sums = [], [], []
    copies = 7 * len(CHUNKS)
    for first, second in GROUPS:
        copies += 2 * (SIZE[first] - 1) + SIZE[first] * (SIZE[second] - 1)
    for _, rows, axes in UNITS:
        first = SIZE[axes[1]] * OWN
        for axis, count in zip(axes, (first, OWN)):
            recv.append(pltpu.VMEM((2, SIZE[axis] - 1, count, rows // 2, TV), bf))
            stage.append(pltpu.VMEM((2, 2, count, rows // 2, TV), bf))
            copies += 2 * (SIZE[axis] - 1)
        sums.append(pltpu.VMEM((first, rows, TV), bf))
    sems = [pltpu.SemaphoreType.DMA((copies,)), pltpu.SemaphoreType.DMA((copies,)), pltpu.SemaphoreType.DMA((K // 2,))]
    return shapes + recv + stage + sums + sems


def per_device(amplitudes, tile_mask, integrals, block_tiles, block_keep, slot_tile):
    masked = amplitudes[0] * tile_mask[0].astype(jnp.bfloat16)[:, :, None]
    rows, tile_count, depth = masked.shape
    vmem, smem = pl.BlockSpec(memory_space=pltpu.VMEM), pl.BlockSpec(memory_space=pltpu.SMEM)
    ladder = pl.pallas_call(
        kernel,
        out_shape=jax.ShapeDtypeStruct((OWN, ROWS, TV), jnp.bfloat16),
        in_specs=[vmem, pl.BlockSpec(memory_space=pl.ANY), smem, smem, smem],
        out_specs=vmem,
        scratch_shapes=scratch_shapes(),
        compiler_params=pltpu.CompilerParams(collective_id=0, has_side_effects=True, vmem_limit_bytes=67043328),
        name="ladder",
    )(masked.reshape(rows * tile_count, depth), integrals, block_tiles, block_keep, slot_tile)
    return ladder[:, None]


def solution(mesh):
    torus = Mesh(mesh.devices.reshape(NZ, NX, NY, NC), ("z", "x", "y", "c"))
    blk, pair = ("z", "x"), ("y", "c")
    return jax.shard_map(
        per_device,
        mesh=torus,
        in_specs=(P(pair, blk, None, None), P(pair, blk, None), P(blk, pair, None), P(blk, None), P(blk), P()),
        out_specs=P(blk, pair, None, None),
        check_vma=False,
    )
```

```python
import jax
import jax.numpy as jnp
from jax import lax
from jax.experimental import pallas as pl
from jax.experimental.pallas import tpu as pltpu
from jax.sharding import Mesh
from jax.sharding import PartitionSpec as P

TV = 128
NT = 12
DW = 8
BW = 8
K = 8
D = DW * TV
ROWS = 384
NZ, NX, NY, NC = 8, 4, 4, 2
OWN = 3
PIECE = NT * NT
ROUTES = ((0, 384, ("x", "z")), (384, 640, ("z", "x")))
ZERO = K * BW
MESH = pl.DeviceIdType.MESH
SIZE = {"z": NZ, "x": NX, "y": NY, "c": NC}

UNITS = (
    (0, 64, ("z", "x")),
    (64, 128, ("x", "z")),
    (192, 96, ("z", "x")),
    (288, 96, ("x", "z")),
)
RANK_PASS = (1.0, 1.0)
AFTER_ALL = (["a11.2.0"], [])
RANK_FIRST = (0.0, 1.0, 2.0, 3.0)
RANK_SECOND = (4.0, 5.0, 6.0, 7.0)
CHUNKS = (
    (0, 0, 2, 1), (0, 2, 2, -1), (0, 4, 2, 1), (0, 6, 2, -1),
    (1, 0, 2, 1), (1, 2, 2, -1), (1, 4, 1, 1), (1, 5, 1, -1), (1, 6, 1, 1), (1, 7, 1, -1),
)

RATE = {"z": 41e3, "x": 41e3, "y": 41e3, "c": 150e3}
AHEAD = 3.0
DELAY = {"z": 2.0, "x": 2.0, "y": 2.0, "c": 1.0}


class Plan:
    def __init__(self):
        self.tasks = []
        self.copies = {}

    def copy(self, name, axis, step, size, src, dst, got):
        self.copies[name] = (len(self.copies), axis, step, size, src, dst, got)

    def task(self, name, needs, run, sends, cost, rank=0.0):
        self.tasks.append((name, tuple(needs), run, tuple(sends), cost, rank))

    def order(self):
        known, waiting, listing, free, now = {}, list(self.tasks), [], {}, 0.0
        while waiting:
            best = None
            for place, task in enumerate(waiting):
                if all(need in known for need in task[1]):
                    when = max([known[need] for need in task[1]] + [now])
                    for name in task[3]:
                        _, axis, step, _, _, _, _ = self.copies[name]
                        when = max(when, free.get((axis, step), 0.0) - AHEAD)
                    key = (when, task[5], place)
                    if best is None or key < best:
                        best = key
            when, _, place = best
            task = waiting.pop(place)
            now = when + task[4]
            known[task[0]] = now
            listing.append(task)
            for name in task[3]:
                _, axis, step, size, _, _, _ = self.copies[name]
                begin = max(now, free.get((axis, step), 0.0))
                free[axis, step] = begin + size / RATE[axis]
                known[name] = free[axis, step] + DELAY[axis]
        return listing, now


def messages(n, step):
    mine = 0 if step > 0 else 1
    listing = [(n // 2, mine)]
    for distance in range(n // 2 - 1, 0, -1):
        listing += [(distance, 1 - mine), (distance, mine)]
    return listing


def kernel(amps, integ, tiles, keep, slots, out, fresh, own_i, raw, every, prod, final, perm, turn, last, before, source, *rest):
    n_units = len(UNITS)
    recvs, stages, sums = rest[: 2 * n_units], rest[2 * n_units : 4 * n_units], rest[4 * n_units : 5 * n_units]
    send_sem, recv_sem, load_sem = rest[5 * n_units :]
    me = {axis: lax.axis_index(axis) for axis in SIZE}
    z, x, y, c = me["z"], me["x"], me["y"], me["c"]

    def shifted(axis, amount):
        return lax.rem(me[axis] + (amount + SIZE[axis]), SIZE[axis])

    loads = []
    for k in range(0, K, 2):
        load = pltpu.make_async_copy(integ.at[pl.ds(k, 2)], fresh.at[pl.ds(k, 2)], load_sem.at[k // 2])
        load.start()
        loads.append(load)

    barrier = pltpu.get_barrier_semaphore()
    for axis, amount in (("z", 1), ("z", -1), ("x", 1), ("x", -1), ("y", 1), ("y", -1), ("c", 1)):
        pl.semaphore_signal(barrier, inc=1, device_id={axis: shifted(axis, amount)}, device_id_type=MESH)
    raw[x, z] = amps[...]
    fr = lax.broadcasted_iota(jnp.int32, (256, 256), 0)
    to = lax.broadcasted_iota(jnp.int32, (256, 256), 1)
    want = ((to >> 6) & 1) * 128 + (to >> 7) * 64 + (to & 63)
    turn[...] = (fr == want).astype(jnp.float32).astype(jnp.bfloat16)
    pl.semaphore_wait(barrier, 7)

    plan = Plan()

    def block(half, first, count, yy, core):
        return own_i.at[half, pl.ds(first, count), 2 * yy + core]

    def split(k):
        loads[k // 2].wait()

        def tile(t, carry):
            kk = k + lax.div(t, 4)
            j = lax.rem(t, 4)
            cols = pl.ds(pl.multiple_of(j * 256, 256), 256)
            moved = jnp.dot(fresh[kk, :, cols], turn[...], preferred_element_type=jnp.float32).astype(jnp.bfloat16)
            place = pl.ds(pl.multiple_of(j * TV, TV), TV)
            own_i[0, kk, 2 * y + c, :, place] = moved[:, :TV]
            own_i[1, kk, 2 * y + c, :, place] = moved[:, TV:]
            return carry

        lax.fori_loop(0, 8, tile, 0)

    for k in range(0, K, 2):
        plan.task(f"split{k}", [], lambda k=k: split(k), [], 0.4, 0.5 + k)

    all_i = []
    for q, (half, first, count, way) in enumerate(CHUNKS):
        size = count * TV * D
        for step in (1, -1):
            plan.copy(f"i{q}{step}", "y", step, size, block(half, first, count, y, c), block(half, first, count, y, c),
                      block(half, first, count, shifted("y", -step), c))
            needs = [f"i{q - 2}{step}"] if q >= 2 else []
            plan.task(f"si{q}{step}", needs + [f"split{first // 2 * 2}"], None, [f"i{q}{step}"], 0.05)
        far = shifted("y", -way)
        plan.copy(f"j{q}", "y", way, size, block(half, first, count, far, c), block(half, first, count, far, c),
                  block(half, first, count, shifted("y", 2), c))
        for tag, yy, need in (("o", y, f"split{first // 2 * 2}"), ("p", shifted("y", -1), f"i{q}1"), ("m", shifted("y", 1), f"i{q}-1"), ("f", shifted("y", 2), f"j{q}")):
            plan.copy(f"c{q}{tag}", "c", 1, size, block(half, first, count, yy, c), block(half, first, count, yy, c),
                      block(half, first, count, yy, 1 - c))
            sends = [f"c{q}{tag}"]
            if tag == ("p" if way == 1 else "m"):
                sends = [f"j{q}"] + sends
            plan.task(f"sc{q}{tag}", [need], None, sends, 0.05, 9.0 if tag == "o" else 0.0)
        all_i.append([f"i{q}1", f"i{q}-1", f"j{q}"] + [f"c{q}{tag}" for tag in "opmf"])

    arrived = {}

    def landed(route, offset, name):
        along = offset[route[2].index("x")]
        arrived.setdefault(NX // 2 if along == -(NX // 2) else along, []).append(name)

    for r, route in enumerate(ROUTES):
        first_lane, lanes, (first, second) = route
        n, m = SIZE[first], SIZE[second]

        def piece(one, two, rows=(0, PIECE), route=route):
            at = dict(zip(route[2], (shifted(route[2][0], one), shifted(route[2][1], two))))
            return raw.at[at["x"], at["z"], pl.ds(rows[0], rows[1] - rows[0]), pl.ds(route[0], route[1])]

        parts = {0: []}
        for step in (1, -1):
            for hop in range(n // 2):
                for half in (0, 1) if hop < n // 2 - 1 else ((0,) if step > 0 else (1,)):
                    name = f"a{r}{step}.{hop}.{half}"
                    rows = ((0, 80), (80, PIECE))[half]
                    ref = piece(-step * hop, 0, rows)
                    plan.copy(name, first, step, (rows[1] - rows[0]) * lanes * 2, ref, ref, piece(-step * (hop + 1), 0, rows))
                    plan.task("s" + name, [f"a{r}{step}.{hop - 1}.{half}"] if hop else [], None, [name], 0.05, 0.0)
                    offset = -step * (hop + 1)
                    parts.setdefault(n // 2 if offset == -(n // 2) else offset, []).append(name)
                    landed(route, (offset, 0), name)
        for number, offset in enumerate(sorted(parts, key=abs)):
            way = 1 if number % 2 == 0 else -1
            for step in (1, -1):
                for hop in range(m // 2 if step == way else m // 2 - 1):
                    name = f"b{r}.{offset}.{step}.{hop}"
                    ref = piece(offset, -step * hop)
                    plan.copy(name, second, step, PIECE * lanes * 2, ref, ref, piece(offset, -step * (hop + 1)))
                    needs = [f"b{r}.{offset}.{step}.{hop - 1}"] if hop else parts[offset] + AFTER_ALL[r]
                    plan.task("s" + name, needs, None, [name], 0.05, RANK_PASS[r] + (0.5 if hop else 0.0) + 0.01 * number)
                    landed(route, (offset, -step * (hop + 1)), name)

    def make_perm():
        to = lax.broadcasted_iota(jnp.int32, (192, 192), 0)
        fr = lax.broadcasted_iota(jnp.int32, (192, 192), 1)
        perm[...] = (fr == (to & 15) * NT + (to >> 4)).astype(jnp.float32).astype(jnp.bfloat16)
        prod[ZERO] = jnp.zeros((ROWS, TV), jnp.bfloat16)

    def make_tables():
        for a in range(NT):
            found = jnp.int32(K)
            for k in range(K):
                found = jnp.where((keep[k] != 0) & (tiles[k, 1] == a), k, found)
            last[a] = found
        for k in range(K):
            found = jnp.int32(K)
            for j in range(k):
                found = jnp.where((keep[j] != 0) & (tiles[j, 1] == tiles[k, 1]), j, found)
            before[k] = found

        def fill(s, carry):
            tile = slots[s]
            found = last[tile >> 3]
            source[s] = jnp.where(found == K, ZERO, found * BW + (tile & 7))
            return carry

        lax.fori_loop(0, NT * BW, fill, 0)

    plan.task("perm", [], make_perm, [], 0.5, 5.0)
    plan.task("tables", [], make_tables, [], 2.0, 90.0)

    def regroup(along):
        there = shifted("x", along)

        def tile(n, carry):
            cols = pl.ds(pl.multiple_of(n * 256, 256), 256)
            for quad in range(NZ // 4):
                for group in range(3):
                    rows = raw[there, 4 * quad : 4 * quad + 4, 48 * group : 48 * group + 48, cols].reshape(192, 256)
                    moved = jnp.dot(perm[...], rows, preferred_element_type=jnp.float32)
                    every[there, quad, group, :, :, cols] = moved.astype(jnp.bfloat16).reshape(NT, 16, 256)
            return carry

        lax.fori_loop(0, D // 256, tile, 0)

    for along, names in arrived.items():
        plan.task(f"regroup{along}", names + ["perm"], lambda along=along: regroup(along), [], 1.5, 3.0)

    def multiply(part, first, count, offsets):
        block = ROWS // NX
        pairs = block // 2
        lane = lax.broadcasted_iota(jnp.int32, (pairs, TV), 1)

        def tile(t, carry):
            k = first + lax.div(t, 2)
            n = lax.rem(t, 2)
            cols = pl.ds(pl.multiple_of(n * 256, 256), 256)
            which = tiles[k, 0]
            blocks = [shifted("x", offset) for offset in offsets]
            lhs = jnp.concatenate([every[at, :, :, which].reshape(block, D) for at in blocks], axis=0)
            value = jnp.dot(lhs, own_i[part, k, :, :, cols].reshape(D, 256), preferred_element_type=jnp.float32)
            found = before[k]
            for number, at in enumerate(blocks):
                rows = pl.ds(pl.multiple_of(part * (ROWS // 2) + at * pairs, 16), pairs)
                for pair in range(2):
                    both = value[number * block : number * block + block, pair * TV : pair * TV + TV]
                    upper, lower = both[:pairs], both[pairs:]
                    packed = (
                        jnp.where(lane < 64, upper, pltpu.roll(lower, 64, 1)),
                        jnp.where(lane < 64, pltpu.roll(upper, 64, 1), lower),
                    )
                    for side in range(2):
                        b = 4 * n + 2 * pair + side
                        old = prod[jnp.where(found == K, ZERO, found * BW + b), rows, :].astype(jnp.float32)
                        prod[k * BW + b, rows, :] = (packed[side] + old).astype(jnp.bfloat16)
            return carry

        lax.fori_loop(0, 2 * count, tile, 0)

    multiplied = {0: [], 1: []}
    near, far = (0, 1, -1), (2,)
    for q, (part, first, count, _) in enumerate(CHUNKS):
        for tag, offsets, cost in (("n", near, 0.65), ("f", far, 0.35)) if part == 0 else (("", near + far, 0.8),):
            needs = all_i[q] + [f"regroup{offset}" for offset in offsets] + ["tables"]
            needs += [name for name in multiplied[part] if name.startswith("mm" + tag)]
            plan.task(f"mm{tag}{q}", needs, lambda a=(part, first, count, offsets): multiply(*a), [], cost * count, 4.0 if tag == "n" else 8.0 * part - 1.0)
            multiplied[part].append(f"mm{tag}{q}")

    def reduce(tag, axis, count, rows, own, recv, stage, sink, need, rank):
        n = SIZE[axis]
        size = count * rows * TV * 2
        for step in (1, -1):
            d = 0 if step > 0 else 1
            listing = messages(n, step)
            for m, (distance, half) in enumerate(listing):
                name = f"{tag}{step}.{distance}.{half}"
                dest = shifted(axis, step * distance)
                upstream = (distance + 1, half)
                if upstream in listing:
                    buf = recv.at[d, listing.index(upstream)]
                    needs = [f"{tag}{step}.{distance + 1}.{half}"]

                    def run(buf=buf, dest=dest, half=half):
                        def one(i, carry):
                            buf[i] = (buf[i].astype(jnp.float32) + own(dest, i, half).astype(jnp.float32)).astype(jnp.bfloat16)
                            return carry

                        lax.fori_loop(0, count, one, 0)
                else:
                    buf = stage.at[d, m]
                    needs = []

                    def run(buf=buf, dest=dest, half=half):
                        def one(i, carry):
                            buf[i] = own(dest, i, half)
                            return carry

                        lax.fori_loop(0, count, one, 0)

                plan.copy(name, axis, step, size, buf, recv.at[d, m], recv.at[d, m])
                plan.task("s" + name, needs + need, run, [name], count * rows / 2000.0, rank)
        index = {step: messages(n, step) for step in (1, -1)}
        for half in range(2):
            def run(half=half):
                def one(i, carry):
                    total = own(me[axis], i, half).astype(jnp.float32)
                    total += recv[0, index[1].index((1, half)), i].astype(jnp.float32)
                    total += recv[1, index[-1].index((1, half)), i].astype(jnp.float32)
                    sink(i, half, total.astype(jnp.bfloat16))
                    return carry

                lax.fori_loop(0, count, one, 0)

            plan.task(f"f{tag}{half}", [f"{tag}1.1.{half}", f"{tag}-1.1.{half}"] + need, run, [], count * rows / 1500.0, rank)
        return [f"f{tag}0", f"f{tag}1"]

    finals = []
    for u, (row, rows, axes) in enumerate(UNITS):
        half_rows = rows // 2
        summed = sums[u]

        if axes[0] == "z":
            count = NX * OWN

            def own1(dest, i, half, row=row, h=half_rows):
                return prod[source[dest * (NX * OWN) + i], row + half * h : row + half * h + h, :]
        else:
            count = NZ * OWN

            def own1(dest, i, half, row=row, h=half_rows):
                slot = lax.div(i, OWN) * (NX * OWN) + dest * OWN + lax.rem(i, OWN)
                return prod[source[slot], row + half * h : row + half * h + h, :]

        def sink1(i, half, value, summed=summed, h=half_rows):
            summed[i, half * h : half * h + h, :] = value

        def own2(dest, i, half, summed=summed, h=half_rows):
            return summed[dest * OWN + i, half * h : half * h + h, :]

        def sink2(i, half, value, row=row, h=half_rows):
            final[i, row + half * h : row + half * h + h, :] = value

        done = reduce(f"r{u}", axes[0], count, half_rows, own1, recvs[2 * u], stages[2 * u], sink1, multiplied[row // (ROWS // 2)], RANK_FIRST[u])
        finals += reduce(f"t{u}", axes[1], OWN, half_rows, own2, recvs[2 * u + 1], stages[2 * u + 1], sink2, done, RANK_SECOND[u])

    def finish():
        to = lax.broadcasted_iota(jnp.int32, (ROWS, ROWS), 0)
        p = lax.broadcasted_iota(jnp.int32, (ROWS, ROWS), 1)
        v = lax.rem(p, ROWS // 2)
        xx, i = lax.div(v, 48), lax.rem(v, 48)
        zz = lax.div(p, ROWS // 2) * 4 + ((i >> 2) & 3)
        natural = zz * (NX * NT) + xx * NT + (i >> 4) * 4 + (i & 3)
        place = (to == natural).astype(jnp.float32).astype(jnp.bfloat16)
        lane = lax.broadcasted_iota(jnp.int32, (ROWS // 2, TV), 1)
        for j in range(OWN):
            left = final[j, : ROWS // 2].astype(jnp.float32)
            right = final[j, ROWS // 2 :].astype(jnp.float32)
            upper = jnp.where(lane < 64, left, pltpu.roll(right, 64, 1))
            lower = jnp.where(lane < 64, pltpu.roll(left, 64, 1), right)
            whole = jnp.concatenate([upper, lower], axis=0).astype(jnp.bfloat16)
            out[j] = jnp.dot(place, whole, preferred_element_type=jnp.float32).astype(jnp.bfloat16)

    plan.task("finish", finals, finish, [], 1.0)

    listing, _ = plan.order()
    waited = set()

    def handle(name, received):
        number, axis, step, _, src, dst, got = plan.copies[name]
        return pltpu.make_async_remote_copy(
            src_ref=src, dst_ref=got if received else dst, send_sem=send_sem.at[number], recv_sem=recv_sem.at[number],
            device_id={axis: shifted(axis, step)}, device_id_type=MESH)

    for _, needs, run, sends, _, _ in listing:
        for need in needs:
            if need in plan.copies and need not in waited:
                waited.add(need)
                handle(need, True).wait_recv()
        if run is not None:
            run()
        for name in sends:
            handle(name, False).start()
    for name in plan.copies:
        if name not in waited:
            handle(name, True).wait_recv()
        handle(name, False).wait_send()


def scratch_shapes():
    bf = jnp.bfloat16
    shapes = [
        pltpu.VMEM((K, TV, D), bf),
        pltpu.VMEM((2, K, DW, TV, D // 2), bf),
        pltpu.VMEM((NX, NZ, PIECE, D), bf),
        pltpu.VMEM((NX, NZ // 4, 3, NT, 16, D), bf),
        pltpu.VMEM((ZERO + 1, ROWS, TV), bf),
        pltpu.VMEM((OWN, ROWS, TV), bf),
        pltpu.VMEM((192, 192), bf),
        pltpu.VMEM((256, 256), bf),
        pltpu.SMEM((NT,), jnp.int32),
        pltpu.SMEM((K,), jnp.int32),
        pltpu.SMEM((NT * BW,), jnp.int32),
    ]
    recv, stage, sums = [], [], []
    copies = 7 * len(CHUNKS)
    for _, _, (first, second) in ROUTES:
        copies += 2 * (SIZE[first] - 1) + SIZE[first] * (SIZE[second] - 1)
    for _, rows, axes in UNITS:
        first = SIZE[axes[1]] * OWN
        for axis, count in zip(axes, (first, OWN)):
            recv.append(pltpu.VMEM((2, SIZE[axis] - 1, count, rows // 2, TV), bf))
            stage.append(pltpu.VMEM((2, 2, count, rows // 2, TV), bf))
            copies += 2 * (SIZE[axis] - 1)
        sums.append(pltpu.VMEM((first, rows, TV), bf))
    sems = [pltpu.SemaphoreType.DMA((copies,)), pltpu.SemaphoreType.DMA((copies,)), pltpu.SemaphoreType.DMA((K // 2,))]
    return shapes + recv + stage + sums + sems


def per_device(amplitudes, tile_mask, integrals, block_tiles, block_keep, slot_tile):
    masked = amplitudes[0] * tile_mask[0].astype(jnp.bfloat16)[:, :, None]
    rows, tile_count, depth = masked.shape
    vmem, smem = pl.BlockSpec(memory_space=pltpu.VMEM), pl.BlockSpec(memory_space=pltpu.SMEM)
    ladder = pl.pallas_call(
        kernel,
        out_shape=jax.ShapeDtypeStruct((OWN, ROWS, TV), jnp.bfloat16),
        in_specs=[vmem, pl.BlockSpec(memory_space=pl.ANY), smem, smem, smem],
        out_specs=vmem,
        scratch_shapes=scratch_shapes(),
        compiler_params=pltpu.CompilerParams(collective_id=0, has_side_effects=True, vmem_limit_bytes=67043328),
        name="ladder",
    )(masked.reshape(rows * tile_count, depth), integrals, block_tiles, block_keep, slot_tile)
    return ladder[:, None]


def solution(mesh):
    torus = Mesh(mesh.devices.reshape(NZ, NX, NY, NC), ("z", "x", "y", "c"))
    blk, pair = ("z", "x"), ("y", "c")
    return jax.shard_map(
        per_device,
        mesh=torus,
        in_specs=(P(pair, blk, None, None), P(pair, blk, None), P(blk, pair, None), P(blk, None), P(blk), P()),
        out_specs=P(blk, pair, None, None),
        check_vma=False,
    )
```

```python
import jax
import jax.numpy as jnp
from jax import lax
from jax.experimental import pallas as pl
from jax.experimental.pallas import tpu as pltpu
from jax.sharding import Mesh
from jax.sharding import PartitionSpec as P

TV = 128
NT = 12
DW = 8
BW = 8
K = 8
D = DW * TV
ROWS = 384
NZ, NX, NY, NC = 8, 4, 4, 2
OWN = 3
PIECE = NT * NT
ROUTES = ((0, 384, ("x", "z")), (384, 640, ("z", "x")))
ZERO = K * BW
MESH = pl.DeviceIdType.MESH
SIZE = {"z": NZ, "x": NX, "y": NY, "c": NC}

UNITS = (
    (0, 64, ("x", "z")),
    (64, 64, ("z", "x")),
    (128, 64, ("x", "z")),
    (192, 64, ("x", "z")),
    (256, 32, ("x", "z")),
    (288, 96, ("z", "x")),
)
RANK_PASS = (1.0, 1.0)
AFTER_ALL = ([], [])
RANK_FIRST = (0.0, 1.0, 2.0, 3.0, 4.0, 5.0)
RANK_SECOND = (3.5, 4.5, 5.5, 6.5, 7.5, 8.5)
CHUNKS = (
    (0, 0, 2, 1), (0, 2, 2, -1), (0, 4, 2, 1), (0, 6, 2, -1),
    (1, 0, 2, 1), (1, 2, 2, -1), (1, 4, 1, 1), (1, 5, 1, -1), (1, 6, 1, 1), (1, 7, 1, -1),
)

RATE = {"z": 41e3, "x": 41e3, "y": 41e3, "c": 150e3}
AHEAD = 3.0
DELAY = {"z": 2.0, "x": 2.0, "y": 2.0, "c": 1.0}


class Plan:
    def __init__(self):
        self.tasks = []
        self.copies = {}

    def copy(self, name, axis, step, size, src, dst, got):
        self.copies[name] = (len(self.copies), axis, step, size, src, dst, got)

    def task(self, name, needs, run, sends, cost, rank=0.0):
        self.tasks.append((name, tuple(needs), run, tuple(sends), cost, rank))

    def order(self):
        known, waiting, listing, free, now = {}, list(self.tasks), [], {}, 0.0
        while waiting:
            best = None
            for place, task in enumerate(waiting):
                if all(need in known for need in task[1]):
                    when = max([known[need] for need in task[1]] + [now])
                    for name in task[3]:
                        _, axis, step, _, _, _, _ = self.copies[name]
                        when = max(when, free.get((axis, step), 0.0) - AHEAD)
                    key = (when, task[5], place)
                    if best is None or key < best:
                        best = key
            when, _, place = best
            task = waiting.pop(place)
            now = when + task[4]
            known[task[0]] = now
            listing.append(task)
            for name in task[3]:
                _, axis, step, size, _, _, _ = self.copies[name]
                begin = max(now, free.get((axis, step), 0.0))
                free[axis, step] = begin + size / RATE[axis]
                known[name] = free[axis, step] + DELAY[axis]
        return listing, now


def messages(n, step):
    mine = 0 if step > 0 else 1
    listing = [(n // 2, mine)]
    for distance in range(n // 2 - 1, 0, -1):
        listing += [(distance, 1 - mine), (distance, mine)]
    return listing


def kernel(amps, integ, tiles, keep, slots, out, fresh, own_i, raw, every, prod, final, perm, turn, last, before, source, *rest):
    n_units = len(UNITS)
    recvs, stages, sums = rest[: 2 * n_units], rest[2 * n_units : 4 * n_units], rest[4 * n_units : 5 * n_units]
    send_sem, recv_sem, load_sem = rest[5 * n_units :]
    me = {axis: lax.axis_index(axis) for axis in SIZE}
    z, x, y, c = me["z"], me["x"], me["y"], me["c"]

    def shifted(axis, amount):
        return lax.rem(me[axis] + (amount + SIZE[axis]), SIZE[axis])

    loads = []
    for k in range(0, K, 2):
        load = pltpu.make_async_copy(integ.at[pl.ds(k, 2)], fresh.at[pl.ds(k, 2)], load_sem.at[k // 2])
        load.start()
        loads.append(load)

    barrier = pltpu.get_barrier_semaphore()
    for axis, amount in (("z", 1), ("z", -1), ("x", 1), ("x", -1), ("y", 1), ("y", -1), ("c", 1)):
        pl.semaphore_signal(barrier, inc=1, device_id={axis: shifted(axis, amount)}, device_id_type=MESH)
    raw[x, z] = amps[...]
    fr = lax.broadcasted_iota(jnp.int32, (256, 256), 0)
    to = lax.broadcasted_iota(jnp.int32, (256, 256), 1)
    want = ((to >> 6) & 1) * 128 + (to >> 7) * 64 + (to & 63)
    turn[...] = (fr == want).astype(jnp.float32).astype(jnp.bfloat16)
    pl.semaphore_wait(barrier, 7)

    plan = Plan()

    def block(half, first, count, yy, core):
        return own_i.at[half, pl.ds(first, count), 2 * yy + core]

    def split(k):
        loads[k // 2].wait()

        def tile(t, carry):
            kk = k + lax.div(t, 4)
            j = lax.rem(t, 4)
            cols = pl.ds(pl.multiple_of(j * 256, 256), 256)
            moved = jnp.dot(fresh[kk, :, cols], turn[...], preferred_element_type=jnp.float32).astype(jnp.bfloat16)
            place = pl.ds(pl.multiple_of(j * TV, TV), TV)
            own_i[0, kk, 2 * y + c, :, place] = moved[:, :TV]
            own_i[1, kk, 2 * y + c, :, place] = moved[:, TV:]
            return carry

        lax.fori_loop(0, 8, tile, 0)

    for k in range(0, K, 2):
        plan.task(f"split{k}", [], lambda k=k: split(k), [], 0.4, 0.5 + k)

    all_i = []
    for q, (half, first, count, way) in enumerate(CHUNKS):
        size = count * TV * D
        for step in (1, -1):
            plan.copy(f"i{q}{step}", "y", step, size, block(half, first, count, y, c), block(half, first, count, y, c),
                      block(half, first, count, shifted("y", -step), c))
            needs = [f"i{q - 2}{step}"] if q >= 2 else []
            plan.task(f"si{q}{step}", needs + [f"split{first // 2 * 2}"], None, [f"i{q}{step}"], 0.05)
        far = shifted("y", -way)
        plan.copy(f"j{q}", "y", way, size, block(half, first, count, far, c), block(half, first, count, far, c),
                  block(half, first, count, shifted("y", 2), c))
        for tag, yy, need in (("o", y, f"split{first // 2 * 2}"), ("p", shifted("y", -1), f"i{q}1"), ("m", shifted("y", 1), f"i{q}-1"), ("f", shifted("y", 2), f"j{q}")):
            plan.copy(f"c{q}{tag}", "c", 1, size, block(half, first, count, yy, c), block(half, first, count, yy, c),
                      block(half, first, count, yy, 1 - c))
            sends = [f"c{q}{tag}"]
            if tag == ("p" if way == 1 else "m"):
                sends = [f"j{q}"] + sends
            plan.task(f"sc{q}{tag}", [need], None, sends, 0.05, 9.0 if tag == "o" else 0.0)
        all_i.append([f"i{q}1", f"i{q}-1", f"j{q}"] + [f"c{q}{tag}" for tag in "opmf"])

    arrived = {}

    def landed(route, offset, name):
        along = offset[route[2].index("x")]
        arrived.setdefault(NX // 2 if along == -(NX // 2) else along, []).append(name)

    for r, route in enumerate(ROUTES):
        first_lane, lanes, (first, second) = route
        n, m = SIZE[first], SIZE[second]

        def piece(one, two, rows=(0, PIECE), route=route):
            at = dict(zip(route[2], (shifted(route[2][0], one), shifted(route[2][1], two))))
            return raw.at[at["x"], at["z"], pl.ds(rows[0], rows[1] - rows[0]), pl.ds(route[0], route[1])]

        parts = {0: []}
        for step in (1, -1):
            for hop in range(n // 2):
                for half in (0, 1) if hop < n // 2 - 1 else ((0,) if step > 0 else (1,)):
                    name = f"a{r}{step}.{hop}.{half}"
                    rows = ((0, 80), (80, PIECE))[half]
                    ref = piece(-step * hop, 0, rows)
                    plan.copy(name, first, step, (rows[1] - rows[0]) * lanes * 2, ref, ref, piece(-step * (hop + 1), 0, rows))
                    plan.task("s" + name, [f"a{r}{step}.{hop - 1}.{half}"] if hop else [], None, [name], 0.05, 0.0)
                    offset = -step * (hop + 1)
                    parts.setdefault(n // 2 if offset == -(n // 2) else offset, []).append(name)
                    landed(route, (offset, 0), name)
        for number, offset in enumerate(sorted(parts, key=abs)):
            way = 1 if number % 2 == 0 else -1
            for step in (1, -1):
                for hop in range(m // 2 if step == way else m // 2 - 1):
                    name = f"b{r}.{offset}.{step}.{hop}"
                    ref = piece(offset, -step * hop)
                    plan.copy(name, second, step, PIECE * lanes * 2, ref, ref, piece(offset, -step * (hop + 1)))
                    needs = [f"b{r}.{offset}.{step}.{hop - 1}"] if hop else parts[offset] + AFTER_ALL[r]
                    plan.task("s" + name, needs, None, [name], 0.05, RANK_PASS[r] + (0.5 if hop else 0.0) + 0.01 * number)
                    landed(route, (offset, -step * (hop + 1)), name)

    def make_perm():
        to = lax.broadcasted_iota(jnp.int32, (192, 192), 0)
        fr = lax.broadcasted_iota(jnp.int32, (192, 192), 1)
        perm[...] = (fr == (to & 15) * NT + (to >> 4)).astype(jnp.float32).astype(jnp.bfloat16)
        prod[ZERO] = jnp.zeros((ROWS, TV), jnp.bfloat16)

    def make_tables():
        for a in range(NT):
            found = jnp.int32(K)
            for k in range(K):
                found = jnp.where((keep[k] != 0) & (tiles[1, k] == a), k, found)
            last[a] = found
        for k in range(K):
            found = jnp.int32(K)
            for j in range(k):
                found = jnp.where((keep[j] != 0) & (tiles[1, j] == tiles[1, k]), j, found)
            before[k] = found

        def fill(s, carry):
            tile = slots[s]
            found = last[tile >> 3]
            source[s] = jnp.where(found == K, ZERO, found * BW + (tile & 7))
            return carry

        lax.fori_loop(0, NT * BW, fill, 0)

    plan.task("perm", [], make_perm, [], 0.5, 5.0)
    plan.task("tables", [], make_tables, [], 2.0, 90.0)

    def regroup(along):
        there = shifted("x", along)

        def tile(n, carry):
            cols = pl.ds(pl.multiple_of(n * 256, 256), 256)
            for quad in range(NZ // 4):
                for group in range(3):
                    rows = raw[there, 4 * quad : 4 * quad + 4, 48 * group : 48 * group + 48, cols].reshape(192, 256)
                    moved = jnp.dot(perm[...], rows, preferred_element_type=jnp.float32)
                    every[there, quad, group, :, :, cols] = moved.astype(jnp.bfloat16).reshape(NT, 16, 256)
            return carry

        lax.fori_loop(0, D // 256, tile, 0)

    for along, names in arrived.items():
        plan.task(f"regroup{along}", names + ["perm"], lambda along=along: regroup(along), [], 1.5, 3.0)

    def multiply(part, first, count, offsets):
        block = ROWS // NX
        pairs = block // 2
        lane = lax.broadcasted_iota(jnp.int32, (pairs, TV), 1)

        def tile(t, carry):
            k = first + lax.div(t, 2)
            n = lax.rem(t, 2)
            cols = pl.ds(pl.multiple_of(n * 256, 256), 256)
            which = tiles[0, k]
            blocks = [shifted("x", offset) for offset in offsets]
            lhs = jnp.concatenate([every[at, :, :, which].reshape(block, D) for at in blocks], axis=0)
            value = jnp.dot(lhs, own_i[part, k, :, :, cols].reshape(D, 256), preferred_element_type=jnp.float32)
            found = before[k]
            for number, at in enumerate(blocks):
                rows = pl.ds(pl.multiple_of(part * (ROWS // 2) + at * pairs, 16), pairs)
                for pair in range(2):
                    both = value[number * block : number * block + block, pair * TV : pair * TV + TV]
                    upper, lower = both[:pairs], both[pairs:]
                    packed = (
                        jnp.where(lane < 64, upper, pltpu.roll(lower, 64, 1)),
                        jnp.where(lane < 64, pltpu.roll(upper, 64, 1), lower),
                    )
                    for side in range(2):
                        b = 4 * n + 2 * pair + side
                        old = prod[jnp.where(found == K, ZERO, found * BW + b), rows, :].astype(jnp.float32)
                        prod[k * BW + b, rows, :] = (packed[side] + old).astype(jnp.bfloat16)
            return carry

        lax.fori_loop(0, 2 * count, tile, 0)

    multiplied = {0: [], 1: []}
    near, far = (0, 1, -1), (2,)
    for q, (part, first, count, _) in enumerate(CHUNKS):
        for tag, offsets, cost in (("n", near, 0.65), ("f", far, 0.35)) if part == 0 else (("", near + far, 0.8),):
            needs = all_i[q] + [f"regroup{offset}" for offset in offsets] + ["tables"]
            needs += [name for name in multiplied[part] if name.startswith("mm" + tag)]
            plan.task(f"mm{tag}{q}", needs, lambda a=(part, first, count, offsets): multiply(*a), [], cost * count, 4.0 if tag == "n" else 8.0 * part - 1.0)
            multiplied[part].append(f"mm{tag}{q}")

    def reduce(tag, axis, count, rows, own, recv, stage, sink, need, rank):
        n = SIZE[axis]
        size = count * rows * TV * 2
        for step in (1, -1):
            d = 0 if step > 0 else 1
            listing = messages(n, step)
            for m, (distance, half) in enumerate(listing):
                name = f"{tag}{step}.{distance}.{half}"
                dest = shifted(axis, step * distance)
                upstream = (distance + 1, half)
                if upstream in listing:
                    buf = recv.at[d, listing.index(upstream)]
                    needs = [f"{tag}{step}.{distance + 1}.{half}"]

                    def run(buf=buf, dest=dest, half=half):
                        def one(i, carry):
                            buf[i] = (buf[i].astype(jnp.float32) + own(dest, i, half).astype(jnp.float32)).astype(jnp.bfloat16)
                            return carry

                        lax.fori_loop(0, count, one, 0)
                else:
                    buf = stage.at[d, m]
                    needs = []

                    def run(buf=buf, dest=dest, half=half):
                        def one(i, carry):
                            buf[i] = own(dest, i, half)
                            return carry

                        lax.fori_loop(0, count, one, 0)

                plan.copy(name, axis, step, size, buf, recv.at[d, m], recv.at[d, m])
                plan.task("s" + name, needs + need, run, [name], count * rows / 2000.0, rank)
        index = {step: messages(n, step) for step in (1, -1)}
        for half in range(2):
            def run(half=half):
                def one(i, carry):
                    total = own(me[axis], i, half).astype(jnp.float32)
                    total += recv[0, index[1].index((1, half)), i].astype(jnp.float32)
                    total += recv[1, index[-1].index((1, half)), i].astype(jnp.float32)
                    sink(i, half, total.astype(jnp.bfloat16))
                    return carry

                lax.fori_loop(0, count, one, 0)

            plan.task(f"f{tag}{half}", [f"{tag}1.1.{half}", f"{tag}-1.1.{half}"] + need, run, [], count * rows / 1500.0, rank)
        return [f"f{tag}0", f"f{tag}1"]

    finals = []
    for u, (row, rows, axes) in enumerate(UNITS):
        half_rows = rows // 2
        summed = sums[u]

        if axes[0] == "z":
            count = NX * OWN

            def own1(dest, i, half, row=row, h=half_rows):
                return prod[source[dest * (NX * OWN) + i], row + half * h : row + half * h + h, :]
        else:
            count = NZ * OWN

            def own1(dest, i, half, row=row, h=half_rows):
                slot = lax.div(i, OWN) * (NX * OWN) + dest * OWN + lax.rem(i, OWN)
                return prod[source[slot], row + half * h : row + half * h + h, :]

        def sink1(i, half, value, summed=summed, h=half_rows):
            summed[i, half * h : half * h + h, :] = value

        def own2(dest, i, half, summed=summed, h=half_rows):
            return summed[dest * OWN + i, half * h : half * h + h, :]

        def sink2(i, half, value, row=row, h=half_rows):
            final[i, row + half * h : row + half * h + h, :] = value

        done = reduce(f"r{u}", axes[0], count, half_rows, own1, recvs[2 * u], stages[2 * u], sink1, multiplied[row // (ROWS // 2)], RANK_FIRST[u])
        finals += reduce(f"t{u}", axes[1], OWN, half_rows, own2, recvs[2 * u + 1], stages[2 * u + 1], sink2, done, RANK_SECOND[u])

    def finish():
        to = lax.broadcasted_iota(jnp.int32, (ROWS, ROWS), 0)
        p = lax.broadcasted_iota(jnp.int32, (ROWS, ROWS), 1)
        v = lax.rem(p, ROWS // 2)
        xx, i = lax.div(v, 48), lax.rem(v, 48)
        zz = lax.div(p, ROWS // 2) * 4 + ((i >> 2) & 3)
        natural = zz * (NX * NT) + xx * NT + (i >> 4) * 4 + (i & 3)
        place = (to == natural).astype(jnp.float32).astype(jnp.bfloat16)
        lane = lax.broadcasted_iota(jnp.int32, (ROWS // 2, TV), 1)
        for j in range(OWN):
            left = final[j, : ROWS // 2].astype(jnp.float32)
            right = final[j, ROWS // 2 :].astype(jnp.float32)
            upper = jnp.where(lane < 64, left, pltpu.roll(right, 64, 1))
            lower = jnp.where(lane < 64, pltpu.roll(left, 64, 1), right)
            whole = jnp.concatenate([upper, lower], axis=0).astype(jnp.bfloat16)
            out[j] = jnp.dot(place, whole, preferred_element_type=jnp.float32).astype(jnp.bfloat16)

    plan.task("finish", finals, finish, [], 1.0)

    listing, _ = plan.order()
    waited = set()

    def handle(name, received):
        number, axis, step, _, src, dst, got = plan.copies[name]
        return pltpu.make_async_remote_copy(
            src_ref=src, dst_ref=got if received else dst, send_sem=send_sem.at[number], recv_sem=recv_sem.at[number],
            device_id={axis: shifted(axis, step)}, device_id_type=MESH)

    for _, needs, run, sends, _, _ in listing:
        for need in needs:
            if need in plan.copies and need not in waited:
                waited.add(need)
                handle(need, True).wait_recv()
        if run is not None:
            run()
        for name in sends:
            handle(name, False).start()
    for name in plan.copies:
        if name not in waited:
            handle(name, True).wait_recv()
        handle(name, False).wait_send()


def scratch_shapes():
    bf = jnp.bfloat16
    shapes = [
        pltpu.VMEM((K, TV, D), bf),
        pltpu.VMEM((2, K, DW, TV, D // 2), bf),
        pltpu.VMEM((NX, NZ, PIECE, D), bf),
        pltpu.VMEM((NX, NZ // 4, 3, NT, 16, D), bf),
        pltpu.VMEM((ZERO + 1, ROWS, TV), bf),
        pltpu.VMEM((OWN, ROWS, TV), bf),
        pltpu.VMEM((192, 192), bf),
        pltpu.VMEM((256, 256), bf),
        pltpu.SMEM((NT,), jnp.int32),
        pltpu.SMEM((K,), jnp.int32),
        pltpu.SMEM((NT * BW,), jnp.int32),
    ]
    recv, stage, sums = [], [], []
    copies = 7 * len(CHUNKS)
    for _, _, (first, second) in ROUTES:
        copies += 2 * (SIZE[first] - 1) + SIZE[first] * (SIZE[second] - 1)
    for _, rows, axes in UNITS:
        first = SIZE[axes[1]] * OWN
        for axis, count in zip(axes, (first, OWN)):
            recv.append(pltpu.VMEM((2, SIZE[axis] - 1, count, rows // 2, TV), bf))
            stage.append(pltpu.VMEM((2, 2, count, rows // 2, TV), bf))
            copies += 2 * (SIZE[axis] - 1)
        sums.append(pltpu.VMEM((first, rows, TV), bf))
    sems = [pltpu.SemaphoreType.DMA((copies,)), pltpu.SemaphoreType.DMA((copies,)), pltpu.SemaphoreType.DMA((K // 2,))]
    return shapes + recv + stage + sums + sems


def per_device(amplitudes, tile_mask, integrals, block_tiles, block_keep, slot_tile):
    masked = amplitudes[0] * tile_mask[0].astype(jnp.bfloat16)[:, :, None]
    rows, tile_count, depth = masked.shape
    vmem, smem = pl.BlockSpec(memory_space=pltpu.VMEM), pl.BlockSpec(memory_space=pltpu.SMEM)
    ladder = pl.pallas_call(
        kernel,
        out_shape=jax.ShapeDtypeStruct((OWN, ROWS, TV), jnp.bfloat16),
        in_specs=[vmem, pl.BlockSpec(memory_space=pl.ANY), smem, smem, smem],
        out_specs=vmem,
        scratch_shapes=scratch_shapes(),
        compiler_params=pltpu.CompilerParams(collective_id=0, has_side_effects=True, vmem_limit_bytes=67043328),
        name="ladder",
    )(masked.reshape(rows * tile_count, depth), integrals, block_tiles.T, block_keep, slot_tile)
    return ladder[:, None]


def solution(mesh):
    torus = Mesh(mesh.devices.reshape(NZ, NX, NY, NC), ("z", "x", "y", "c"))
    blk, pair = ("z", "x"), ("y", "c")
    return jax.shard_map(
        per_device,
        mesh=torus,
        in_specs=(P(pair, blk, None, None), P(pair, blk, None), P(blk, pair, None), P(blk, None), P(blk), P()),
        out_specs=P(blk, pair, None, None),
        check_vma=False,
    )
```

```python
import jax
import jax.numpy as jnp
from jax import lax
from jax.experimental import pallas as pl
from jax.experimental.pallas import tpu as pltpu
from jax.sharding import Mesh
from jax.sharding import PartitionSpec as P

TV = 128
NT = 12
DW = 8
BW = 8
K = 8
D = DW * TV
ROWS = 384
NZ, NX, NY, NC = 8, 4, 4, 2
OWN = 3
PIECE = NT * NT
ROUTES = ((0, 384, ("x", "z")), (384, 640, ("z", "x")))
ZERO = K * BW
MESH = pl.DeviceIdType.MESH
SIZE = {"z": NZ, "x": NX, "y": NY, "c": NC}

UNITS = (
    (0, 64, ("x", "z")),
    (64, 64, ("z", "x")),
    (128, 64, ("x", "z")),
    (192, 64, ("x", "z")),
    (256, 32, ("x", "z")),
    (288, 96, ("z", "x")),
)
RANK_PASS = (1.0, 1.0)
AFTER_ALL = ([], [])
RANK_FIRST = (0.0, 1.0, 2.0, 3.0, 4.0, 5.0)
RANK_SECOND = (3.5, 4.5, 5.5, 6.5, 7.5, 8.5)
CHUNKS = (
    (0, 0, 2, 1), (0, 2, 2, -1), (0, 4, 2, 1), (0, 6, 2, -1),
    (1, 0, 2, 1), (1, 2, 2, -1), (1, 4, 1, 1), (1, 5, 1, -1), (1, 6, 1, 1), (1, 7, 1, -1),
)

RATE = {"z": 41e3, "x": 41e3, "y": 41e3, "c": 150e3}
AHEAD = 3.0
DELAY = {"z": 2.0, "x": 2.0, "y": 2.0, "c": 1.0}


class Plan:
    def __init__(self):
        self.tasks = []
        self.copies = {}

    def copy(self, name, axis, step, size, src, dst, got):
        self.copies[name] = (len(self.copies), axis, step, size, src, dst, got)

    def task(self, name, needs, run, sends, cost, rank=0.0):
        self.tasks.append((name, tuple(needs), run, tuple(sends), cost, rank))

    def order(self):
        known, waiting, listing, free, now = {}, list(self.tasks), [], {}, 0.0
        while waiting:
            best = None
            for place, task in enumerate(waiting):
                if all(need in known for need in task[1]):
                    when = max([known[need] for need in task[1]] + [now])
                    for name in task[3]:
                        _, axis, step, _, _, _, _ = self.copies[name]
                        when = max(when, free.get((axis, step), 0.0) - AHEAD)
                    key = (when, task[5], place)
                    if best is None or key < best:
                        best = key
            when, _, place = best
            task = waiting.pop(place)
            now = when + task[4]
            known[task[0]] = now
            listing.append(task)
            for name in task[3]:
                _, axis, step, size, _, _, _ = self.copies[name]
                begin = max(now, free.get((axis, step), 0.0))
                free[axis, step] = begin + size / RATE[axis]
                known[name] = free[axis, step] + DELAY[axis]
        return listing, now


def messages(n, step):
    mine = 0 if step > 0 else 1
    listing = [(n // 2, mine)]
    for distance in range(n // 2 - 1, 0, -1):
        listing += [(distance, 1 - mine), (distance, mine)]
    return listing


def kernel(amps, mask, integ, tiles, keep, slots, out, fresh, own_i, raw, every, prod, final, perm, turn, place, last, before, source, *rest):
    n_units = len(UNITS)
    recvs, stages, sums = rest[: 2 * n_units], rest[2 * n_units : 4 * n_units], rest[4 * n_units : 5 * n_units]
    send_sem, recv_sem, load_sem = rest[5 * n_units :]
    me = {axis: lax.axis_index(axis) for axis in SIZE}
    z, x, y, c = me["z"], me["x"], me["y"], me["c"]

    def shifted(axis, amount):
        return lax.rem(me[axis] + (amount + SIZE[axis]), SIZE[axis])

    loads = []
    for k in range(0, K, 2):
        load = pltpu.make_async_copy(integ.at[pl.ds(k, 2)], fresh.at[pl.ds(k, 2)], load_sem.at[k // 2])
        load.start()
        loads.append(load)

    barrier = pltpu.get_barrier_semaphore()
    for axis, amount in (("z", 1), ("z", -1), ("x", 1), ("x", -1), ("y", 1), ("y", -1), ("c", 1)):
        pl.semaphore_signal(barrier, inc=1, device_id={axis: shifted(axis, amount)}, device_id_type=MESH)
    row = lax.broadcasted_iota(jnp.int32, (PIECE, NT), 0)
    col = lax.broadcasted_iota(jnp.int32, (PIECE, NT), 1)
    pick = (lax.div(row, NT) == col).astype(jnp.float32)
    flags = jnp.concatenate([mask[r] for r in range(NT)], axis=0).astype(jnp.float32)
    spread = jnp.dot(pick, flags, preferred_element_type=jnp.float32)
    column = jnp.sum(jnp.where(lax.rem(row, NT) == col, spread, 0.0), axis=1, keepdims=True)
    flat = jnp.concatenate([amps[0, r].astype(jnp.float32) for r in range(NT)], axis=0)
    raw[x, z] = (flat * column).astype(jnp.bfloat16)
    fr = lax.broadcasted_iota(jnp.int32, (256, 256), 0)
    to = lax.broadcasted_iota(jnp.int32, (256, 256), 1)
    want = ((to >> 6) & 1) * 128 + (to >> 7) * 64 + (to & 63)
    turn[...] = (fr == want).astype(jnp.float32).astype(jnp.bfloat16)
    pl.semaphore_wait(barrier, 7)

    plan = Plan()

    def block(half, first, count, yy, core):
        return own_i.at[half, pl.ds(first, count), 2 * yy + core]

    def split(k):
        loads[k // 2].wait()

        def tile(t, carry):
            kk = k + lax.div(t, 4)
            j = lax.rem(t, 4)
            cols = pl.ds(pl.multiple_of(j * 256, 256), 256)
            moved = jnp.dot(fresh[kk, :, cols], turn[...], preferred_element_type=jnp.float32).astype(jnp.bfloat16)
            place = pl.ds(pl.multiple_of(j * TV, TV), TV)
            own_i[0, kk, 2 * y + c, :, place] = moved[:, :TV]
            own_i[1, kk, 2 * y + c, :, place] = moved[:, TV:]
            return carry

        lax.fori_loop(0, 8, tile, 0)

    for k in range(0, K, 2):
        plan.task(f"split{k}", [], lambda k=k: split(k), [], 0.4, 0.5 + k)

    all_i = []
    for q, (half, first, count, way) in enumerate(CHUNKS):
        size = count * TV * D
        for step in (1, -1):
            plan.copy(f"i{q}{step}", "y", step, size, block(half, first, count, y, c), block(half, first, count, y, c),
                      block(half, first, count, shifted("y", -step), c))
            needs = [f"i{q - 2}{step}"] if q >= 2 else []
            plan.task(f"si{q}{step}", needs + [f"split{first // 2 * 2}"], None, [f"i{q}{step}"], 0.05)
        far = shifted("y", -way)
        plan.copy(f"j{q}", "y", way, size, block(half, first, count, far, c), block(half, first, count, far, c),
                  block(half, first, count, shifted("y", 2), c))
        for tag, yy, need in (("o", y, f"split{first // 2 * 2}"), ("p", shifted("y", -1), f"i{q}1"), ("m", shifted("y", 1), f"i{q}-1"), ("f", shifted("y", 2), f"j{q}")):
            plan.copy(f"c{q}{tag}", "c", 1, size, block(half, first, count, yy, c), block(half, first, count, yy, c),
                      block(half, first, count, yy, 1 - c))
            sends = [f"c{q}{tag}"]
            if tag == ("p" if way == 1 else "m"):
                sends = [f"j{q}"] + sends
            plan.task(f"sc{q}{tag}", [need], None, sends, 0.05, 9.0 if tag == "o" else 0.0)
        all_i.append([f"i{q}1", f"i{q}-1", f"j{q}"] + [f"c{q}{tag}" for tag in "opmf"])

    arrived = {}

    def landed(route, offset, name):
        along = offset[route[2].index("x")]
        arrived.setdefault(NX // 2 if along == -(NX // 2) else along, []).append(name)

    for r, route in enumerate(ROUTES):
        first_lane, lanes, (first, second) = route
        n, m = SIZE[first], SIZE[second]

        def piece(one, two, rows=(0, PIECE), route=route):
            at = dict(zip(route[2], (shifted(route[2][0], one), shifted(route[2][1], two))))
            return raw.at[at["x"], at["z"], pl.ds(rows[0], rows[1] - rows[0]), pl.ds(route[0], route[1])]

        parts = {0: []}
        for step in (1, -1):
            for hop in range(n // 2):
                for half in (0, 1) if hop < n // 2 - 1 else ((0,) if step > 0 else (1,)):
                    name = f"a{r}{step}.{hop}.{half}"
                    rows = ((0, 80), (80, PIECE))[half]
                    ref = piece(-step * hop, 0, rows)
                    plan.copy(name, first, step, (rows[1] - rows[0]) * lanes * 2, ref, ref, piece(-step * (hop + 1), 0, rows))
                    plan.task("s" + name, [f"a{r}{step}.{hop - 1}.{half}"] if hop else [], None, [name], 0.05, 0.0)
                    offset = -step * (hop + 1)
                    parts.setdefault(n // 2 if offset == -(n // 2) else offset, []).append(name)
                    landed(route, (offset, 0), name)
        for number, offset in enumerate(sorted(parts, key=abs)):
            way = 1 if number % 2 == 0 else -1
            for step in (1, -1):
                for hop in range(m // 2 if step == way else m // 2 - 1):
                    name = f"b{r}.{offset}.{step}.{hop}"
                    ref = piece(offset, -step * hop)
                    plan.copy(name, second, step, PIECE * lanes * 2, ref, ref, piece(offset, -step * (hop + 1)))
                    needs = [f"b{r}.{offset}.{step}.{hop - 1}"] if hop else parts[offset] + AFTER_ALL[r]
                    plan.task("s" + name, needs, None, [name], 0.05, RANK_PASS[r] + (0.5 if hop else 0.0) + 0.01 * number)
                    landed(route, (offset, -step * (hop + 1)), name)

    def make_perm():
        to = lax.broadcasted_iota(jnp.int32, (192, 192), 0)
        fr = lax.broadcasted_iota(jnp.int32, (192, 192), 1)
        perm[...] = (fr == (to & 15) * NT + (to >> 4)).astype(jnp.float32).astype(jnp.bfloat16)
        prod[ZERO] = jnp.zeros((ROWS, TV), jnp.bfloat16)

    def make_tables():
        for a in range(NT):
            found = jnp.int32(K)
            for k in range(K):
                found = jnp.where((keep[k] != 0) & (tiles[1, k] == a), k, found)
            last[a] = found
        for k in range(K):
            found = jnp.int32(K)
            for j in range(k):
                found = jnp.where((keep[j] != 0) & (tiles[1, j] == tiles[1, k]), j, found)
            before[k] = found

        def fill(s, carry):
            tile = slots[s]
            found = last[tile >> 3]
            source[s] = jnp.where(found == K, ZERO, found * BW + (tile & 7))
            return carry

        lax.fori_loop(0, NT * BW, fill, 0)

    plan.task("perm", [], make_perm, [], 0.5, 5.0)
    plan.task("tables", [], make_tables, [], 2.0, 90.0)

    def regroup(along):
        there = shifted("x", along)

        def tile(n, carry):
            cols = pl.ds(pl.multiple_of(n * 256, 256), 256)
            for quad in range(NZ // 4):
                for group in range(3):
                    rows = raw[there, 4 * quad : 4 * quad + 4, 48 * group : 48 * group + 48, cols].reshape(192, 256)
                    moved = jnp.dot(perm[...], rows, preferred_element_type=jnp.float32)
                    every[there, quad, group, :, :, cols] = moved.astype(jnp.bfloat16).reshape(NT, 16, 256)
            return carry

        lax.fori_loop(0, D // 256, tile, 0)

    for along, names in arrived.items():
        plan.task(f"regroup{along}", names + ["perm"], lambda along=along: regroup(along), [], 1.5, 3.0)

    def multiply(part, first, count, offsets):
        block = ROWS // NX
        pairs = block // 2
        lane = lax.broadcasted_iota(jnp.int32, (pairs, TV), 1)

        def tile(t, carry):
            k = first + lax.div(t, 2)
            n = lax.rem(t, 2)
            cols = pl.ds(pl.multiple_of(n * 256, 256), 256)
            which = tiles[0, k]
            blocks = [shifted("x", offset) for offset in offsets]
            lhs = jnp.concatenate([every[at, :, :, which].reshape(block, D) for at in blocks], axis=0)
            value = jnp.dot(lhs, own_i[part, k, :, :, cols].reshape(D, 256), preferred_element_type=jnp.float32)
            found = before[k]
            for number, at in enumerate(blocks):
                rows = pl.ds(pl.multiple_of(part * (ROWS // 2) + at * pairs, 16), pairs)
                for pair in range(2):
                    both = value[number * block : number * block + block, pair * TV : pair * TV + TV]
                    upper, lower = both[:pairs], both[pairs:]
                    packed = (
                        jnp.where(lane < 64, upper, pltpu.roll(lower, 64, 1)),
                        jnp.where(lane < 64, pltpu.roll(upper, 64, 1), lower),
                    )
                    for side in range(2):
                        b = 4 * n + 2 * pair + side
                        old = prod[jnp.where(found == K, ZERO, found * BW + b), rows, :].astype(jnp.float32)
                        prod[k * BW + b, rows, :] = (packed[side] + old).astype(jnp.bfloat16)
            return carry

        lax.fori_loop(0, 2 * count, tile, 0)

    multiplied = {0: [], 1: []}
    near, far = (0, 1, -1), (2,)
    for q, (part, first, count, _) in enumerate(CHUNKS):
        for tag, offsets, cost in (("n", near, 0.65), ("f", far, 0.35)) if part == 0 else (("", near + far, 0.8),):
            needs = all_i[q] + [f"regroup{offset}" for offset in offsets] + ["tables"]
            needs += [name for name in multiplied[part] if name.startswith("mm" + tag)]
            plan.task(f"mm{tag}{q}", needs, lambda a=(part, first, count, offsets): multiply(*a), [], cost * count, 4.0 if tag == "n" else 8.0 * part - 1.0)
            multiplied[part].append(f"mm{tag}{q}")

    def reduce(tag, axis, count, rows, own, recv, stage, sink, need, rank):
        n = SIZE[axis]
        size = count * rows * TV * 2
        for step in (1, -1):
            d = 0 if step > 0 else 1
            listing = messages(n, step)
            for m, (distance, half) in enumerate(listing):
                name = f"{tag}{step}.{distance}.{half}"
                dest = shifted(axis, step * distance)
                upstream = (distance + 1, half)
                if upstream in listing:
                    buf = recv.at[d, listing.index(upstream)]
                    needs = [f"{tag}{step}.{distance + 1}.{half}"]

                    def run(buf=buf, dest=dest, half=half):
                        def one(i, carry):
                            buf[i] = (buf[i].astype(jnp.float32) + own(dest, i, half).astype(jnp.float32)).astype(jnp.bfloat16)
                            return carry

                        lax.fori_loop(0, count, one, 0)
                else:
                    buf = stage.at[d, m]
                    needs = []

                    def run(buf=buf, dest=dest, half=half):
                        def one(i, carry):
                            buf[i] = own(dest, i, half)
                            return carry

                        lax.fori_loop(0, count, one, 0)

                plan.copy(name, axis, step, size, buf, recv.at[d, m], recv.at[d, m])
                plan.task("s" + name, needs + need, run, [name], count * rows / 2000.0, rank)
        index = {step: messages(n, step) for step in (1, -1)}
        for half in range(2):
            def run(half=half):
                def one(i, carry):
                    total = own(me[axis], i, half).astype(jnp.float32)
                    total += recv[0, index[1].index((1, half)), i].astype(jnp.float32)
                    total += recv[1, index[-1].index((1, half)), i].astype(jnp.float32)
                    sink(i, half, total.astype(jnp.bfloat16))
                    return carry

                lax.fori_loop(0, count, one, 0)

            plan.task(f"f{tag}{half}", [f"{tag}1.1.{half}", f"{tag}-1.1.{half}"] + need, run, [], count * rows / 1500.0, rank)
        return [f"f{tag}0", f"f{tag}1"]

    finals = []
    for u, (row, rows, axes) in enumerate(UNITS):
        half_rows = rows // 2
        summed = sums[u]

        if axes[0] == "z":
            count = NX * OWN

            def own1(dest, i, half, row=row, h=half_rows):
                return prod[source[dest * (NX * OWN) + i], row + half * h : row + half * h + h, :]
        else:
            count = NZ * OWN

            def own1(dest, i, half, row=row, h=half_rows):
                slot = lax.div(i, OWN) * (NX * OWN) + dest * OWN + lax.rem(i, OWN)
                return prod[source[slot], row + half * h : row + half * h + h, :]

        def sink1(i, half, value, summed=summed, h=half_rows):
            summed[i, half * h : half * h + h, :] = value

        def own2(dest, i, half, summed=summed, h=half_rows):
            return summed[dest * OWN + i, half * h : half * h + h, :]

        def sink2(i, half, value, row=row, h=half_rows):
            final[i, row + half * h : row + half * h + h, :] = value

        done = reduce(f"r{u}", axes[0], count, half_rows, own1, recvs[2 * u], stages[2 * u], sink1, multiplied[row // (ROWS // 2)], RANK_FIRST[u])
        finals += reduce(f"t{u}", axes[1], OWN, half_rows, own2, recvs[2 * u + 1], stages[2 * u + 1], sink2, done, RANK_SECOND[u])

    def make_place():
        to = lax.broadcasted_iota(jnp.int32, (ROWS, ROWS), 0)
        p = lax.broadcasted_iota(jnp.int32, (ROWS, ROWS), 1)
        v = lax.rem(p, ROWS // 2)
        xx, i = lax.div(v, 48), lax.rem(v, 48)
        zz = lax.div(p, ROWS // 2) * 4 + ((i >> 2) & 3)
        natural = zz * (NX * NT) + xx * NT + (i >> 4) * 4 + (i & 3)
        place[...] = (to == natural).astype(jnp.float32).astype(jnp.bfloat16)

    plan.task("place", [], make_place, [], 1.0, 95.0)

    def finish():
        lane = lax.broadcasted_iota(jnp.int32, (ROWS // 2, TV), 1)
        for j in range(OWN):
            left = final[j, : ROWS // 2].astype(jnp.float32)
            right = final[j, ROWS // 2 :].astype(jnp.float32)
            upper = jnp.where(lane < 64, left, pltpu.roll(right, 64, 1))
            lower = jnp.where(lane < 64, pltpu.roll(left, 64, 1), right)
            whole = jnp.concatenate([upper, lower], axis=0).astype(jnp.bfloat16)
            out[j] = jnp.dot(place[...], whole, preferred_element_type=jnp.float32).astype(jnp.bfloat16)

    plan.task("finish", finals + ["place"], finish, [], 1.0)

    listing, _ = plan.order()
    waited = set()

    def handle(name, received):
        number, axis, step, _, src, dst, got = plan.copies[name]
        return pltpu.make_async_remote_copy(
            src_ref=src, dst_ref=got if received else dst, send_sem=send_sem.at[number], recv_sem=recv_sem.at[number],
            device_id={axis: shifted(axis, step)}, device_id_type=MESH)

    for _, needs, run, sends, _, _ in listing:
        for need in needs:
            if need in plan.copies and need not in waited:
                waited.add(need)
                handle(need, True).wait_recv()
        if run is not None:
            run()
        for name in sends:
            handle(name, False).start()
    for name in plan.copies:
        if name not in waited:
            handle(name, True).wait_recv()
        handle(name, False).wait_send()


def scratch_shapes():
    bf = jnp.bfloat16
    shapes = [
        pltpu.VMEM((K, TV, D), bf),
        pltpu.VMEM((2, K, DW, TV, D // 2), bf),
        pltpu.VMEM((NX, NZ, PIECE, D), bf),
        pltpu.VMEM((NX, NZ // 4, 3, NT, 16, D), bf),
        pltpu.VMEM((ZERO + 1, ROWS, TV), bf),
        pltpu.VMEM((OWN, ROWS, TV), bf),
        pltpu.VMEM((192, 192), bf),
        pltpu.VMEM((256, 256), bf),
        pltpu.VMEM((ROWS, ROWS), bf),
        pltpu.SMEM((NT,), jnp.int32),
        pltpu.SMEM((K,), jnp.int32),
        pltpu.SMEM((NT * BW,), jnp.int32),
    ]
    recv, stage, sums = [], [], []
    copies = 7 * len(CHUNKS)
    for _, _, (first, second) in ROUTES:
        copies += 2 * (SIZE[first] - 1) + SIZE[first] * (SIZE[second] - 1)
    for _, rows, axes in UNITS:
        first = SIZE[axes[1]] * OWN
        for axis, count in zip(axes, (first, OWN)):
            recv.append(pltpu.VMEM((2, SIZE[axis] - 1, count, rows // 2, TV), bf))
            stage.append(pltpu.VMEM((2, 2, count, rows // 2, TV), bf))
            copies += 2 * (SIZE[axis] - 1)
        sums.append(pltpu.VMEM((first, rows, TV), bf))
    sems = [pltpu.SemaphoreType.DMA((copies,)), pltpu.SemaphoreType.DMA((copies,)), pltpu.SemaphoreType.DMA((K // 2,))]
    return shapes + recv + stage + sums + sems


def per_device(amplitudes, tile_mask, integrals, block_tiles, block_keep, slot_tile):
    vmem, smem = pl.BlockSpec(memory_space=pltpu.VMEM), pl.BlockSpec(memory_space=pltpu.SMEM)
    ladder = pl.pallas_call(
        kernel,
        out_shape=jax.ShapeDtypeStruct((OWN, ROWS, TV), jnp.bfloat16),
        in_specs=[vmem, vmem, pl.BlockSpec(memory_space=pl.ANY), smem, smem, smem],
        out_specs=vmem,
        scratch_shapes=scratch_shapes(),
        compiler_params=pltpu.CompilerParams(collective_id=0, has_side_effects=True, vmem_limit_bytes=67043328),
        name="ladder",
    )(amplitudes, tile_mask.transpose(1, 0, 2), integrals, block_tiles.T, block_keep, slot_tile)
    return ladder[:, None]


def solution(mesh):
    torus = Mesh(mesh.devices.reshape(NZ, NX, NY, NC), ("z", "x", "y", "c"))
    blk, pair = ("z", "x"), ("y", "c")
    return jax.shard_map(
        per_device,
        mesh=torus,
        in_specs=(P(pair, blk, None, None), P(pair, blk, None), P(blk, pair, None), P(blk, None), P(blk), P()),
        out_specs=P(blk, pair, None, None),
        check_vma=False,
    )
```

```python
import jax
import jax.numpy as jnp
from jax import lax
from jax.experimental import pallas as pl
from jax.experimental.pallas import tpu as pltpu
from jax.sharding import Mesh
from jax.sharding import PartitionSpec as P

TV = 128
NT = 12
DW = 8
BW = 8
K = 8
D = DW * TV
ROWS = 384
NZ, NX, NY, NC = 8, 4, 4, 2
OWN = 3
PIECE = NT * NT
ROUTES = ((0, 384, ("x", "z")), (384, 640, ("z", "x")))
ZERO = K * BW
MESH = pl.DeviceIdType.MESH
SIZE = {"z": NZ, "x": NX, "y": NY, "c": NC}

UNITS = (
    (0, 32, ("x", "z")),
    (32, 96, ("x", "z")),
    (128, 64, ("z", "x")),
    (192, 64, ("x", "z")),
    (256, 32, ("x", "z")),
    (288, 96, ("z", "x")),
)
RANK_PASS = (1.0, 1.0)
AFTER_ALL = ([], [])
RANK_FIRST = (-1.2, 2.2, 3.2, 1.8, 2.8, 5.0)
RANK_SECOND = (0.3, 3.7, 4.7, 3.3, 4.3, 6.5)
CHUNKS = (
    (0, 0, 2, 1), (0, 2, 2, -1), (0, 4, 2, 1), (0, 6, 2, -1),
    (1, 0, 2, 1), (1, 2, 2, -1), (1, 4, 1, 1), (1, 5, 1, -1), (1, 6, 1, 1), (1, 7, 1, -1),
)

RATE = {"z": 41e3, "x": 41e3, "y": 41e3, "c": 150e3}
AHEAD = 3.0
DELAY = {"z": 2.0, "x": 2.0, "y": 2.0, "c": 1.0}


class Plan:
    def __init__(self):
        self.tasks = []
        self.copies = {}

    def copy(self, name, axis, step, size, src, dst, got):
        self.copies[name] = (len(self.copies), axis, step, size, src, dst, got)

    def task(self, name, needs, run, sends, cost, rank=0.0):
        self.tasks.append((name, tuple(needs), run, tuple(sends), cost, rank))

    def order(self):
        known, waiting, listing, free, now = {}, list(self.tasks), [], {}, 0.0
        while waiting:
            best = None
            for place, task in enumerate(waiting):
                if all(need in known for need in task[1]):
                    when = max([known[need] for need in task[1]] + [now])
                    for name in task[3]:
                        _, axis, step, _, _, _, _ = self.copies[name]
                        when = max(when, free.get((axis, step), 0.0) - AHEAD)
                    key = (when, task[5], place)
                    if best is None or key < best:
                        best = key
            when, _, place = best
            task = waiting.pop(place)
            now = when + task[4]
            known[task[0]] = now
            listing.append(task)
            for name in task[3]:
                _, axis, step, size, _, _, _ = self.copies[name]
                begin = max(now, free.get((axis, step), 0.0))
                free[axis, step] = begin + size / RATE[axis]
                known[name] = free[axis, step] + DELAY[axis]
        return listing, now


def messages(n, step):
    mine = 0 if step > 0 else 1
    listing = [(n // 2, mine)]
    for distance in range(n // 2 - 1, 0, -1):
        listing += [(distance, 1 - mine), (distance, mine)]
    return listing


def kernel(amps, mask, integ, tiles, keep, slots, out, fresh, own_i, raw, every, prod, final, perm, turn, place, last, before, source, *rest):
    n_units = len(UNITS)
    recvs, stages, sums = rest[: 2 * n_units], rest[2 * n_units : 4 * n_units], rest[4 * n_units : 5 * n_units]
    send_sem, recv_sem, load_sem = rest[5 * n_units :]
    me = {axis: lax.axis_index(axis) for axis in SIZE}
    z, x, y, c = me["z"], me["x"], me["y"], me["c"]

    def shifted(axis, amount):
        return lax.rem(me[axis] + (amount + SIZE[axis]), SIZE[axis])

    loads = []
    for k in range(0, K, 2):
        load = pltpu.make_async_copy(integ.at[pl.ds(k, 2)], fresh.at[pl.ds(k, 2)], load_sem.at[k // 2])
        load.start()
        loads.append(load)

    barrier = pltpu.get_barrier_semaphore()
    for axis, amount in (("z", 1), ("z", -1), ("x", 1), ("x", -1), ("y", 1), ("y", -1), ("c", 1)):
        pl.semaphore_signal(barrier, inc=1, device_id={axis: shifted(axis, amount)}, device_id_type=MESH)
    row = lax.broadcasted_iota(jnp.int32, (PIECE, NT), 0)
    col = lax.broadcasted_iota(jnp.int32, (PIECE, NT), 1)
    pick = (lax.div(row, NT) == col).astype(jnp.float32)
    flags = jnp.concatenate([mask[r] for r in range(NT)], axis=0).astype(jnp.float32)
    spread = jnp.dot(pick, flags, preferred_element_type=jnp.float32)
    column = jnp.sum(jnp.where(lax.rem(row, NT) == col, spread, 0.0), axis=1, keepdims=True)
    flat = jnp.concatenate([amps[0, r].astype(jnp.float32) for r in range(NT)], axis=0)
    raw[x, z] = (flat * column).astype(jnp.bfloat16)
    fr = lax.broadcasted_iota(jnp.int32, (256, 256), 0)
    to = lax.broadcasted_iota(jnp.int32, (256, 256), 1)
    want = ((to >> 6) & 1) * 128 + (to >> 7) * 64 + (to & 63)
    turn[...] = (fr == want).astype(jnp.float32).astype(jnp.bfloat16)
    pl.semaphore_wait(barrier, 7)

    plan = Plan()

    def block(half, first, count, yy, core):
        return own_i.at[half, pl.ds(first, count), 2 * yy + core]

    def split(k):
        loads[k // 2].wait()

        def tile(t, carry):
            kk = k + lax.div(t, 4)
            j = lax.rem(t, 4)
            cols = pl.ds(pl.multiple_of(j * 256, 256), 256)
            moved = jnp.dot(fresh[kk, :, cols], turn[...], preferred_element_type=jnp.float32).astype(jnp.bfloat16)
            place = pl.ds(pl.multiple_of(j * TV, TV), TV)
            own_i[0, kk, 2 * y + c, :, place] = moved[:, :TV]
            own_i[1, kk, 2 * y + c, :, place] = moved[:, TV:]
            return carry

        lax.fori_loop(0, 8, tile, 0)

    for k in range(0, K, 2):
        plan.task(f"split{k}", [], lambda k=k: split(k), [], 0.4, 0.5 + k)

    all_i = []
    for q, (half, first, count, way) in enumerate(CHUNKS):
        size = count * TV * D
        for step in (1, -1):
            plan.copy(f"i{q}{step}", "y", step, size, block(half, first, count, y, c), block(half, first, count, y, c),
                      block(half, first, count, shifted("y", -step), c))
            needs = [f"i{q - 2}{step}"] if q >= 2 else []
            plan.task(f"si{q}{step}", needs + [f"split{first // 2 * 2}"], None, [f"i{q}{step}"], 0.05)
        far = shifted("y", -way)
        plan.copy(f"j{q}", "y", way, size, block(half, first, count, far, c), block(half, first, count, far, c),
                  block(half, first, count, shifted("y", 2), c))
        for tag, yy, need in (("o", y, f"split{first // 2 * 2}"), ("p", shifted("y", -1), f"i{q}1"), ("m", shifted("y", 1), f"i{q}-1"), ("f", shifted("y", 2), f"j{q}")):
            plan.copy(f"c{q}{tag}", "c", 1, size, block(half, first, count, yy, c), block(half, first, count, yy, c),
                      block(half, first, count, yy, 1 - c))
            sends = [f"c{q}{tag}"]
            if tag == ("p" if way == 1 else "m"):
                sends = [f"j{q}"] + sends
            plan.task(f"sc{q}{tag}", [need], None, sends, 0.05, 9.0 if tag == "o" else 0.0)
        all_i.append([f"i{q}1", f"i{q}-1", f"j{q}"] + [f"c{q}{tag}" for tag in "opmf"])

    arrived = {}

    def landed(route, offset, name):
        along = offset[route[2].index("x")]
        arrived.setdefault(NX // 2 if along == -(NX // 2) else along, []).append(name)

    for r, route in enumerate(ROUTES):
        first_lane, lanes, (first, second) = route
        n, m = SIZE[first], SIZE[second]

        def piece(one, two, rows=(0, PIECE), route=route):
            at = dict(zip(route[2], (shifted(route[2][0], one), shifted(route[2][1], two))))
            return raw.at[at["x"], at["z"], pl.ds(rows[0], rows[1] - rows[0]), pl.ds(route[0], route[1])]

        parts = {0: []}
        for step in (1, -1):
            for hop in range(n // 2):
                for half in (0, 1) if hop < n // 2 - 1 else ((0,) if step > 0 else (1,)):
                    name = f"a{r}{step}.{hop}.{half}"
                    rows = ((0, 80), (80, PIECE))[half]
                    ref = piece(-step * hop, 0, rows)
                    plan.copy(name, first, step, (rows[1] - rows[0]) * lanes * 2, ref, ref, piece(-step * (hop + 1), 0, rows))
                    plan.task("s" + name, [f"a{r}{step}.{hop - 1}.{half}"] if hop else [], None, [name], 0.05, 0.0)
                    offset = -step * (hop + 1)
                    parts.setdefault(n // 2 if offset == -(n // 2) else offset, []).append(name)
                    landed(route, (offset, 0), name)
        for number, offset in enumerate(sorted(parts, key=abs)):
            way = 1 if number % 2 == 0 else -1
            for step in (1, -1):
                for hop in range(m // 2 if step == way else m // 2 - 1):
                    name = f"b{r}.{offset}.{step}.{hop}"
                    ref = piece(offset, -step * hop)
                    plan.copy(name, second, step, PIECE * lanes * 2, ref, ref, piece(offset, -step * (hop + 1)))
                    needs = [f"b{r}.{offset}.{step}.{hop - 1}"] if hop else parts[offset] + AFTER_ALL[r]
                    plan.task("s" + name, needs, None, [name], 0.05, RANK_PASS[r] + (0.5 if hop else 0.0) + 0.01 * number)
                    landed(route, (offset, -step * (hop + 1)), name)

    def make_perm():
        to = lax.broadcasted_iota(jnp.int32, (192, 192), 0)
        fr = lax.broadcasted_iota(jnp.int32, (192, 192), 1)
        perm[...] = (fr == (to & 15) * NT + (to >> 4)).astype(jnp.float32).astype(jnp.bfloat16)
        prod[ZERO] = jnp.zeros((ROWS, TV), jnp.bfloat16)

    def make_tables():
        for a in range(NT):
            found = jnp.int32(K)
            for k in range(K):
                found = jnp.where((keep[k] != 0) & (tiles[1, k] == a), k, found)
            last[a] = found
        for k in range(K):
            found = jnp.int32(K)
            for j in range(k):
                found = jnp.where((keep[j] != 0) & (tiles[1, j] == tiles[1, k]), j, found)
            before[k] = found

        def fill(s, carry):
            tile = slots[s]
            found = last[tile >> 3]
            source[s] = jnp.where(found == K, ZERO, found * BW + (tile & 7))
            return carry

        lax.fori_loop(0, NT * BW, fill, 0)

    plan.task("perm", [], make_perm, [], 0.5, 5.0)
    plan.task("tables", [], make_tables, [], 2.0, 90.0)

    def regroup(along):
        there = shifted("x", along)

        def tile(n, carry):
            cols = pl.ds(pl.multiple_of(n * 256, 256), 256)
            for quad in range(NZ // 4):
                for group in range(3):
                    rows = raw[there, 4 * quad : 4 * quad + 4, 48 * group : 48 * group + 48, cols].reshape(192, 256)
                    moved = jnp.dot(perm[...], rows, preferred_element_type=jnp.float32)
                    every[there, quad, group, :, :, cols] = moved.astype(jnp.bfloat16).reshape(NT, 16, 256)
            return carry

        lax.fori_loop(0, D // 256, tile, 0)

    for along, names in arrived.items():
        plan.task(f"regroup{along}", names + ["perm"], lambda along=along: regroup(along), [], 1.5, 3.0)

    def multiply(part, first, count, offsets):
        block = ROWS // NX
        pairs = block // 2
        lane = lax.broadcasted_iota(jnp.int32, (pairs, TV), 1)

        def tile(t, carry):
            k = first + lax.div(t, 2)
            n = lax.rem(t, 2)
            cols = pl.ds(pl.multiple_of(n * 256, 256), 256)
            which = tiles[0, k]
            blocks = [shifted("x", offset) for offset in offsets]
            lhs = jnp.concatenate([every[at, :, :, which].reshape(block, D) for at in blocks], axis=0)
            value = jnp.dot(lhs, own_i[part, k, :, :, cols].reshape(D, 256), preferred_element_type=jnp.float32)
            found = before[k]
            for number, at in enumerate(blocks):
                rows = pl.ds(pl.multiple_of(part * (ROWS // 2) + at * pairs, 16), pairs)
                for pair in range(2):
                    both = value[number * block : number * block + block, pair * TV : pair * TV + TV]
                    upper, lower = both[:pairs], both[pairs:]
                    packed = (
                        jnp.where(lane < 64, upper, pltpu.roll(lower, 64, 1)),
                        jnp.where(lane < 64, pltpu.roll(upper, 64, 1), lower),
                    )
                    for side in range(2):
                        b = 4 * n + 2 * pair + side
                        old = prod[jnp.where(found == K, ZERO, found * BW + b), rows, :].astype(jnp.float32)
                        prod[k * BW + b, rows, :] = (packed[side] + old).astype(jnp.bfloat16)
            return carry

        lax.fori_loop(0, 2 * count, tile, 0)

    multiplied = {0: [], 1: []}
    near, far = (0, 1, -1), (2,)
    for q, (part, first, count, _) in enumerate(CHUNKS):
        for tag, offsets, cost in (("n", near, 0.65), ("f", far, 0.35)) if part == 0 else (("", near + far, 0.8),):
            needs = all_i[q] + [f"regroup{offset}" for offset in offsets] + ["tables"]
            needs += [name for name in multiplied[part] if name.startswith("mm" + tag)]
            plan.task(f"mm{tag}{q}", needs, lambda a=(part, first, count, offsets): multiply(*a), [], cost * count, 4.0 if tag == "n" else 8.0 * part - 1.0)
            multiplied[part].append(f"mm{tag}{q}")

    def reduce(tag, axis, count, rows, own, recv, stage, sink, need, rank):
        n = SIZE[axis]
        size = count * rows * TV * 2
        for step in (1, -1):
            d = 0 if step > 0 else 1
            listing = messages(n, step)
            for m, (distance, half) in enumerate(listing):
                name = f"{tag}{step}.{distance}.{half}"
                dest = shifted(axis, step * distance)
                upstream = (distance + 1, half)
                if upstream in listing:
                    buf = recv.at[d, listing.index(upstream)]
                    needs = [f"{tag}{step}.{distance + 1}.{half}"]

                    def run(buf=buf, dest=dest, half=half):
                        def one(i, carry):
                            buf[i] = (buf[i].astype(jnp.float32) + own(dest, i, half).astype(jnp.float32)).astype(jnp.bfloat16)
                            return carry

                        lax.fori_loop(0, count, one, 0)
                else:
                    buf = stage.at[d, m]
                    needs = []

                    def run(buf=buf, dest=dest, half=half):
                        def one(i, carry):
                            buf[i] = own(dest, i, half)
                            return carry

                        lax.fori_loop(0, count, one, 0)

                plan.copy(name, axis, step, size, buf, recv.at[d, m], recv.at[d, m])
                plan.task("s" + name, needs + need, run, [name], count * rows / 2000.0, rank)
        index = {step: messages(n, step) for step in (1, -1)}
        for half in range(2):
            def run(half=half):
                def one(i, carry):
                    total = own(me[axis], i, half).astype(jnp.float32)
                    total += recv[0, index[1].index((1, half)), i].astype(jnp.float32)
                    total += recv[1, index[-1].index((1, half)), i].astype(jnp.float32)
                    sink(i, half, total.astype(jnp.bfloat16))
                    return carry

                lax.fori_loop(0, count, one, 0)

            plan.task(f"f{tag}{half}", [f"{tag}1.1.{half}", f"{tag}-1.1.{half}"] + need, run, [], count * rows / 1500.0, rank)
        return [f"f{tag}0", f"f{tag}1"]

    finals = []
    for u, (row, rows, axes) in enumerate(UNITS):
        half_rows = rows // 2
        summed = sums[u]

        if axes[0] == "z":
            count = NX * OWN

            def own1(dest, i, half, row=row, h=half_rows):
                return prod[source[dest * (NX * OWN) + i], row + half * h : row + half * h + h, :]
        else:
            count = NZ * OWN

            def own1(dest, i, half, row=row, h=half_rows):
                slot = lax.div(i, OWN) * (NX * OWN) + dest * OWN + lax.rem(i, OWN)
                return prod[source[slot], row + half * h : row + half * h + h, :]

        def sink1(i, half, value, summed=summed, h=half_rows):
            summed[i, half * h : half * h + h, :] = value

        def own2(dest, i, half, summed=summed, h=half_rows):
            return summed[dest * OWN + i, half * h : half * h + h, :]

        def sink2(i, half, value, row=row, h=half_rows):
            final[i, row + half * h : row + half * h + h, :] = value

        done = reduce(f"r{u}", axes[0], count, half_rows, own1, recvs[2 * u], stages[2 * u], sink1, multiplied[row // (ROWS // 2)], RANK_FIRST[u])
        finals += reduce(f"t{u}", axes[1], OWN, half_rows, own2, recvs[2 * u + 1], stages[2 * u + 1], sink2, done, RANK_SECOND[u])

    def make_place():
        to = lax.broadcasted_iota(jnp.int32, (ROWS, ROWS), 0)
        p = lax.broadcasted_iota(jnp.int32, (ROWS, ROWS), 1)
        v = lax.rem(p, ROWS // 2)
        xx, i = lax.div(v, 48), lax.rem(v, 48)
        zz = lax.div(p, ROWS // 2) * 4 + ((i >> 2) & 3)
        natural = zz * (NX * NT) + xx * NT + (i >> 4) * 4 + (i & 3)
        place[...] = (to == natural).astype(jnp.float32).astype(jnp.bfloat16)

    plan.task("place", [], make_place, [], 1.0, 95.0)

    def finish():
        lane = lax.broadcasted_iota(jnp.int32, (ROWS // 2, TV), 1)
        for j in range(OWN):
            left = final[j, : ROWS // 2].astype(jnp.float32)
            right = final[j, ROWS // 2 :].astype(jnp.float32)
            upper = jnp.where(lane < 64, left, pltpu.roll(right, 64, 1))
            lower = jnp.where(lane < 64, pltpu.roll(left, 64, 1), right)
            whole = jnp.concatenate([upper, lower], axis=0).astype(jnp.bfloat16)
            out[j] = jnp.dot(place[...], whole, preferred_element_type=jnp.float32).astype(jnp.bfloat16)

    plan.task("finish", finals + ["place"], finish, [], 1.0)

    listing, _ = plan.order()
    waited = set()

    def handle(name, received):
        number, axis, step, _, src, dst, got = plan.copies[name]
        return pltpu.make_async_remote_copy(
            src_ref=src, dst_ref=got if received else dst, send_sem=send_sem.at[number], recv_sem=recv_sem.at[number],
            device_id={axis: shifted(axis, step)}, device_id_type=MESH)

    for _, needs, run, sends, _, _ in listing:
        for need in needs:
            if need in plan.copies and need not in waited:
                waited.add(need)
                handle(need, True).wait_recv()
        if run is not None:
            run()
        for name in sends:
            handle(name, False).start()
    for name in plan.copies:
        if name not in waited:
            handle(name, True).wait_recv()
        handle(name, False).wait_send()


def scratch_shapes():
    bf = jnp.bfloat16
    shapes = [
        pltpu.VMEM((K, TV, D), bf),
        pltpu.VMEM((2, K, DW, TV, D // 2), bf),
        pltpu.VMEM((NX, NZ, PIECE, D), bf),
        pltpu.VMEM((NX, NZ // 4, 3, NT, 16, D), bf),
        pltpu.VMEM((ZERO + 1, ROWS, TV), bf),
        pltpu.VMEM((OWN, ROWS, TV), bf),
        pltpu.VMEM((192, 192), bf),
        pltpu.VMEM((256, 256), bf),
        pltpu.VMEM((ROWS, ROWS), bf),
        pltpu.SMEM((NT,), jnp.int32),
        pltpu.SMEM((K,), jnp.int32),
        pltpu.SMEM((NT * BW,), jnp.int32),
    ]
    recv, stage, sums = [], [], []
    copies = 7 * len(CHUNKS)
    for _, _, (first, second) in ROUTES:
        copies += 2 * (SIZE[first] - 1) + SIZE[first] * (SIZE[second] - 1)
    for _, rows, axes in UNITS:
        first = SIZE[axes[1]] * OWN
        for axis, count in zip(axes, (first, OWN)):
            recv.append(pltpu.VMEM((2, SIZE[axis] - 1, count, rows // 2, TV), bf))
            stage.append(pltpu.VMEM((2, 2, count, rows // 2, TV), bf))
            copies += 2 * (SIZE[axis] - 1)
        sums.append(pltpu.VMEM((first, rows, TV), bf))
    sems = [pltpu.SemaphoreType.DMA((copies,)), pltpu.SemaphoreType.DMA((copies,)), pltpu.SemaphoreType.DMA((K // 2,))]
    return shapes + recv + stage + sums + sems


def per_device(amplitudes, tile_mask, integrals, block_tiles, block_keep, slot_tile):
    vmem, smem = pl.BlockSpec(memory_space=pltpu.VMEM), pl.BlockSpec(memory_space=pltpu.SMEM)
    ladder = pl.pallas_call(
        kernel,
        out_shape=jax.ShapeDtypeStruct((OWN, ROWS, TV), jnp.bfloat16),
        in_specs=[vmem, vmem, pl.BlockSpec(memory_space=pl.ANY), smem, smem, smem],
        out_specs=vmem,
        scratch_shapes=scratch_shapes(),
        compiler_params=pltpu.CompilerParams(collective_id=0, has_side_effects=True, vmem_limit_bytes=67043328),
        name="ladder",
    )(amplitudes, tile_mask.transpose(1, 0, 2), integrals, block_tiles.T, block_keep, slot_tile)
    return ladder[:, None]


def solution(mesh):
    torus = Mesh(mesh.devices.reshape(NZ, NX, NY, NC), ("z", "x", "y", "c"))
    blk, pair = ("z", "x"), ("y", "c")
    return jax.shard_map(
        per_device,
        mesh=torus,
        in_specs=(P(pair, blk, None, None), P(pair, blk, None), P(blk, pair, None), P(blk, None), P(blk), P()),
        out_specs=P(blk, pair, None, None),
        check_vma=False,
    )
```
